32 devices in a mesh: batch: 4 (over x, core), hidden: 4 (over z), solver: 2 (over y).
Axes of the slice: x: 2, y: 2, z: 4, core: 2. Of those that a mesh axis runs over, the one named last changes fastest.
Arguments:
- activations: bfloat16 [1024, 4096], P('batch', ('hidden', 'solver')), may hold values from -16 to 16, as said below
- cotangent: bfloat16 [8192, 1024], P(('hidden', 'solver'), 'batch'), may hold values from -0.1875 to 0.1875
- weight: bfloat16 [4096, 8192], P(('hidden', 'solver'), 'batch'), may hold values from -0.09375 to 0.09375
- left_old: float32 [4, 8, 1024, 1024], P('hidden', 'batch'), may hold values from -0.001953125 to 2.0019531, as said below
- right_old: float32 [4, 8, 1024, 1024], P('hidden', 'batch'), may hold values from -0.001953125 to 2.0019531, as said below
Outputs:
- first_out: bfloat16 [8192, 1024], P(('hidden', 'solver'), 'batch')
- new_left: float32 [4, 8, 1024, 1024], P('hidden', 'batch', 'solver')
- new_right: float32 [4, 8, 1024, 1024], P('hidden', 'batch', 'solver')
- direction: float32 [4096, 8192], P(('hidden', 'solver'), 'batch')
- second_out: bfloat16 [8192, 1024], P(('hidden', 'solver'), 'batch')
The draws below stay inside these ranges and needn't reach their ends.
Inputs may be any that keep to these rules, and one draw needn't show every extreme that they name: `activations`: in the hidden draw each feature carries its own scale. `left_old`: every block is symmetric, its diagonal is positive and larger than the sum of the magnitudes of the rest of its row. `right_old`: every block is symmetric, its diagonal is positive and larger than the sum of the magnitudes of the rest of its row.
All inputs are finite; a program needn't handle non-finite values. Where the reference program divides by a largest or mean magnitude, that divisor is 1e-20 or more.
Results may differ from the reference program's by a relative error of at most 0.017.
Values may be sent and summed in bfloat16 or wider, within the bound.
A program may use at most 128 MiB of HBM per device.

```python
import jax
import jax.numpy as jnp
from jax import lax

DIN = 4096
DOUT = 8192
BLOCK = 1024
TOK_DEV = 256
TOKENS = 1024
NROW = 4
NCOL = 8
N_BATCH = 4


def draw_activations(key, part):
    values = jnp.clip(jax.random.normal(jax.random.fold_in(key, 11), (TOKENS, DIN), jnp.float32), -4.0, 4.0)
    return values.astype(jnp.bfloat16)


def factor_blocks(key):
    diagonal = jnp.exp(jax.random.uniform(jax.random.fold_in(key, 21), (NROW, NCOL, BLOCK), jnp.float32, jnp.log(0.5), jnp.log(2.0)))
    off_part = jnp.clip(jax.random.normal(jax.random.fold_in(key, 22), (NROW, NCOL, BLOCK, BLOCK), jnp.float32), -4.0, 4.0) * (0.5 / BLOCK)
    symmetric = 0.5 * (off_part + jnp.swapaxes(off_part, 2, 3))
    identity = jnp.eye(BLOCK, dtype=jnp.float32)
    return symmetric * (1.0 - identity) + diagonal[..., None] * identity


def draw_left_old(key, part):
    return factor_blocks(jax.random.fold_in(key, 1))


def draw_right_old(key, part):
    return factor_blocks(jax.random.fold_in(key, 2))


def block_scale(stream_key, shape, shards, least, high):
    factor_of, own = 1.0, jax.random.fold_in(stream_key, 6)
    for axis_at, shards_of in shards:
        heights = jnp.exp(jax.random.uniform(jax.random.fold_in(own, axis_at), (shards_of,), jnp.float32, least / len(shards), high / len(shards)))
        factor_of = factor_of * jnp.repeat(heights, shape[axis_at] // shards_of).reshape([-1 if axis == axis_at else 1 for axis in range(len(shape))])
    return factor_of


def normal_values(stream_key, extent, scale, most, split=(), kind=jnp.bfloat16):
    entries = jax.random.normal(stream_key, extent, jnp.float32) * scale
    if len(split) > 0:
        entries = block_scale(stream_key, extent, split, -0.22, 0.18) * entries
    return jnp.clip(entries, min=-most, max=most).astype(kind)


def setup_inputs(seed: int = 0) -> dict:
    splits = jax.random.split(jax.random.key(seed), 6)
    return {
        "activations": draw_activations(jax.random.fold_in(splits[5], 71), 0),
        "cotangent": normal_values(splits[1], (DOUT, TOKENS), (TOKENS ** -0.5), 0.1875, ((0, 8), (1, 4))),
        "weight": normal_values(splits[2], (DIN, DOUT), DIN ** -0.5, 0.09375, ((0, 8), (1, 4))),
        "left_old": draw_left_old(jax.random.fold_in(splits[5], 71), 0),
        "right_old": draw_right_old(jax.random.fold_in(splits[5], 71), 0),
    }


STAT_DECAY = 0.8
LEARN_RATE = 0.005
EPSILON = 1e-06

def product(left_mat, right_mat):
    return jnp.dot(left_mat, right_mat, precision=lax.Precision.HIGHEST, preferred_element_type=jnp.float32)

def inverse_root(factor):
    identity = jnp.eye(BLOCK, dtype=jnp.float32)
    scaled = 2.5 / (jnp.max(lax.optimization_barrier(jnp.sum(jnp.abs(factor), axis=1))) + EPSILON)
    moment = scaled * factor
    newton_step = (5.0 * identity - moment) * 0.25
    power_term = product(product(product(product(newton_step, newton_step), newton_step), newton_step), moment)
    next_step = (5.0 * identity - power_term) * 0.25
    return scaled ** 0.25 * product(newton_step, next_step)

def forward(activations, weight):
    outputs = lax.dot_general(weight, activations, (((0,), (1,)), ((), ())), preferred_element_type=jnp.float32)
    return outputs.astype(jnp.bfloat16)

def per_block(inputs):
    grad_block, left_block, right_block = inputs
    gram_left = lax.dot_general(grad_block, grad_block, (((0,), (0,)), ((), ())), preferred_element_type=jnp.float32)
    gram_right = lax.dot_general(grad_block, grad_block, (((1,), (1,)), ((), ())), preferred_element_type=jnp.float32)
    left_new = STAT_DECAY * left_block + (1.0 - STAT_DECAY) / BLOCK * gram_left
    right_new = STAT_DECAY * right_block + (1.0 - STAT_DECAY) / BLOCK * gram_right
    grad_float = grad_block.astype(jnp.float32).T
    mixed_rows = product(inverse_root(left_new), grad_float)
    update = product(mixed_rows, inverse_root(right_new))
    spread = jnp.sqrt(jnp.mean(update * update) + EPSILON)
    return (left_new, right_new, update / spread)

def reference(activations, cotangent, weight, left_old, right_old):
    first_out = forward(activations, weight)

    def add_group(carry, group):
        acts = lax.dynamic_slice_in_dim(activations, (group * TOK_DEV).astype(jnp.int32), TOK_DEV, 0)
        cotan = lax.dynamic_slice_in_dim(cotangent, (group * TOK_DEV).astype(jnp.int32), TOK_DEV, 1)
        partial_grad = jnp.dot(cotan, acts, preferred_element_type=jnp.float32)
        return (carry + partial_grad.astype(jnp.bfloat16).astype(jnp.float32), None)
    grad_sum, _ = lax.scan(add_group, jnp.zeros((DOUT, DIN), jnp.float32), jnp.arange(N_BATCH, dtype=jnp.int32))
    grad = grad_sum.astype(jnp.bfloat16)
    blocks = grad.reshape(NCOL, BLOCK, NROW, BLOCK).transpose(2, 0, 1, 3).reshape(NROW * NCOL, BLOCK, BLOCK)
    lefts = left_old.reshape(NROW * NCOL, BLOCK, BLOCK)
    rights = right_old.reshape(NROW * NCOL, BLOCK, BLOCK)
    new_left, new_right, updates = lax.map(per_block, (blocks, lefts, rights))
    new_left = new_left.reshape(NROW, NCOL, BLOCK, BLOCK)
    new_right = new_right.reshape(NROW, NCOL, BLOCK, BLOCK)
    direction = updates.reshape(NROW, NCOL, BLOCK, BLOCK).transpose(0, 2, 1, 3).reshape(DIN, DOUT)
    new_weight = (weight.astype(jnp.float32) - LEARN_RATE * direction).astype(jnp.bfloat16)
    second_out = forward(activations, new_weight)
    return (first_out, new_left, new_right, direction, second_out)
```

```python
import functools

import jax
import jax.numpy as jnp
from jax import lax
from jax.experimental import pallas as pl
from jax.experimental.pallas import tpu as pltpu
from jax.sharding import PartitionSpec as P

BLOCK = 1024


STAT_DECAY = 0.8
LEARN_RATE = 0.005
EPSILON = 1e-06

ALL = ("batch", "hidden", "solver")
FEATURES = ("hidden", "solver")


def product(left_mat, right_mat):
    return jnp.einsum("bij,bjk->bik", left_mat, right_mat, preferred_element_type=jnp.float32)


def prepare(factor):
    identity = jnp.eye(BLOCK, dtype=jnp.float32)
    scaled = 2.5 / (jnp.max(jnp.sum(jnp.abs(factor), axis=2), axis=1) + EPSILON)
    moment = scaled[:, None, None] * factor
    newton_step = (5.0 * identity - moment) * 0.25
    return (scaled, moment.astype(jnp.bfloat16), newton_step.astype(jnp.bfloat16))


def apply_root(start, moment, step):
    power = start
    for _ in range(4):
        power = product(power.astype(jnp.bfloat16), step)
    power = product(power.astype(jnp.bfloat16), moment)
    return (5.0 * start.astype(jnp.float32) - power) * 0.25


def body(activations, cotangent, weight, left_old, right_old, *, n_batch, n_solver, n_feat):
    rows_here = weight.shape[0]
    nblocks = weight.shape[1] // BLOCK
    per_batch = n_feat // n_batch
    out_rows = weight.shape[1] // per_batch
    tokens = activations.shape[0]
    to_owner = [
        (b * n_feat + c * n_batch + t, t * n_feat + b * per_batch + c)
        for b in range(n_batch)
        for c in range(per_batch)
        for t in range(n_batch)
    ]
    from_owner = [(target, source) for source, target in to_owner]

    def partial_forward(weight_here):
        split = weight_here.reshape(rows_here, per_batch, out_rows)
        out = jnp.einsum("fco,btf->cbot", split, acts_all, preferred_element_type=jnp.float32)
        return out.astype(jnp.bfloat16).reshape(n_feat * out_rows, tokens)

    def reduce_forward(partial):
        return lax.psum_scatter(partial, FEATURES, scatter_dimension=0, tiled=True)

    acts_all = lax.all_gather(activations, "batch", axis=0, tiled=False)
    here = lax.axis_index("solver")
    acts_block = jnp.zeros((n_batch, tokens, n_solver * rows_here), acts_all.dtype)
    for shift in range(n_solver):
        part = acts_all
        if shift > 0:
            pairs = [(at, (at + shift) % n_solver) for at in range(n_solver)]
            part = lax.ppermute(acts_all, "solver", pairs)
        first_col = lax.rem(here + n_solver - shift, n_solver) * rows_here
        acts_block = lax.dynamic_update_slice_in_dim(acts_block, part, first_col, 2)
    cot_moved = lax.ppermute(cotangent, ALL, from_owner)
    cot_all = lax.all_gather(cot_moved, FEATURES, axis=0, tiled=False)
    cot_all = cot_all.reshape(per_batch, n_batch, out_rows, tokens)
    first_partial = partial_forward(weight)
    first_partial, cot_all = lax.optimization_barrier((first_partial, cot_all))
    first_sum = reduce_forward(first_partial)
    grad_full = jnp.einsum("cbot,btf->cof", cot_all, acts_block, preferred_element_type=jnp.float32)
    grad_full = grad_full.astype(jnp.bfloat16).reshape(nblocks, BLOCK, BLOCK)
    gram_left = jnp.einsum("bnm,bnk->bmk", grad_full, grad_full, preferred_element_type=jnp.float32)
    gram_right = jnp.einsum(
        "bnm,bkm->bnk", grad_full, grad_full, preferred_element_type=jnp.float32
    )
    left_all = STAT_DECAY * left_old[0] + (1.0 - STAT_DECAY) / BLOCK * gram_left
    right_all = STAT_DECAY * right_old[0] + (1.0 - STAT_DECAY) / BLOCK * gram_right
    first_row = lax.axis_index("solver") * rows_here
    new_left = lax.dynamic_slice_in_dim(left_all, first_row, rows_here, 1)[None]
    new_right = lax.dynamic_slice_in_dim(right_all, first_row, rows_here, 1)[None]
    scale_left, moment_left, step_left = prepare(left_all)
    own_rows = lax.dynamic_slice_in_dim(step_left, first_row, rows_here, 1)
    root_rows = apply_root(own_rows, moment_left, step_left)
    mixed_rows = jnp.einsum(
        "brm,bnm->brn",
        root_rows.astype(jnp.bfloat16),
        grad_full,
        preferred_element_type=jnp.float32,
    )
    scale_right, moment_right, step_right = prepare(right_all)
    turned = product(mixed_rows.astype(jnp.bfloat16), step_right)
    scale_both = (scale_left**0.25) * (scale_right**0.25)
    update = scale_both[:, None, None] * apply_root(turned, moment_right, step_right)
    update, first_sum = lax.optimization_barrier((update, first_sum))
    first_out = lax.ppermute(first_sum, ALL, to_owner)
    squares = lax.psum(jnp.sum(update * update, axis=(1, 2)), "solver")
    spread = jnp.sqrt(squares / (BLOCK * BLOCK) + EPSILON)
    scaled_update = update / spread[:, None, None]
    direction = jnp.transpose(scaled_update, (1, 0, 2)).reshape(rows_here, nblocks * BLOCK)
    new_weight = (weight.astype(jnp.float32) - LEARN_RATE * direction).astype(jnp.bfloat16)
    second_sum = reduce_forward(partial_forward(new_weight))
    second_sum, new_left, new_right = lax.optimization_barrier((second_sum, new_left, new_right))
    second_out = lax.ppermute(second_sum, ALL, to_owner)
    return (first_out, new_left, new_right, direction, second_out)


MESH = pl.DeviceIdType.MESH
VMEM_LIMIT = 62 * 1024 * 1024
PIECES = 4
TILE = 256


def remote(src, dst, send_sem, recv_sem, device):
    return pltpu.make_async_remote_copy(
        src_ref=src,
        dst_ref=dst,
        send_sem=send_sem,
        recv_sem=recv_sem,
        device_id=device,
        device_id_type=MESH,
    )


def position():
    return lax.axis_index("batch"), lax.axis_index("hidden"), lax.axis_index("solver")


def flip(index, bits):
    bit = 1
    while bit <= bits:
        if bits & bit:
            index = index + bit * (1 - 2 * ((index // bit) % 2))
        bit *= 2
    return index


def line_barrier(n_batch, n_line):
    b, h, s = position()
    barrier = pltpu.get_barrier_semaphore()
    for bits in range(1, n_batch):
        pl.semaphore_signal(barrier, inc=1, device_id=(flip(b, bits), h, s), device_id_type=MESH)
    pl.semaphore_signal(barrier, inc=1, device_id=(b, h, 1 - s), device_id_type=MESH)

    @pl.when(h > 0)
    def _():
        pl.semaphore_signal(barrier, inc=1, device_id=(b, h - 1, s), device_id_type=MESH)

    @pl.when(h < n_line - 1)
    def _():
        pl.semaphore_signal(barrier, inc=1, device_id=(b, h + 1, s), device_id_type=MESH)

    ends = (h == 0).astype(jnp.int32) + (h == n_line - 1).astype(jnp.int32)
    pl.semaphore_wait(barrier, n_batch + 2 - ends)


def gather_kernel(
    n_batch,
    n_line,
    acts_ref,
    cot_ref,
    weight_ref,
    grad_ref,
    acts_all,
    weight_all,
    first_ref,
    cot_line,
    cot_all,
    local_sem,
    acts_send,
    acts_recv,
    weight_send,
    weight_recv,
    line_send,
    line_recv,
    swap_send,
    swap_recv,
    swap_local,
):
    b, h, s = position()
    tokens, feats = acts_ref.shape
    outs = cot_ref.shape[0]
    rows = outs // PIECES

    own_cot = pltpu.make_async_copy(cot_ref, cot_line.at[h], local_sem.at[0])

    def acts_slot(bb, ss):
        return acts_all.at[
            pl.ds(pl.multiple_of(bb * tokens, tokens), tokens),
            pl.ds(pl.multiple_of(ss * feats, feats), feats),
        ]

    def weight_from(ss):
        return weight_ref.at[:, pl.ds(pl.multiple_of(ss * outs, outs), outs)]

    def weight_slot(ss):
        return weight_all.at[pl.ds(pl.multiple_of(ss * feats, feats), feats), :]

    own_acts = pltpu.make_async_copy(acts_ref, acts_slot(b, s), local_sem.at[1])
    own_weight = pltpu.make_async_copy(weight_from(s), weight_slot(s), local_sem.at[2])
    own_cot.start()
    own_acts.start()
    own_weight.start()
    line_barrier(n_batch, n_line)
    own_acts.wait()
    own_cot.wait()

    def line_slot(hp, q):
        return cot_line.at[hp, pl.ds(q * rows, rows)]

    def up(hp, q):
        return remote(
            line_slot(hp, q), line_slot(hp, q), line_send.at[0, hp, q], line_recv.at[hp, q], (b, h + 1, s)
        )

    def down(hp, q):
        return remote(
            line_slot(hp, q), line_slot(hp, q), line_send.at[1, hp, q], line_recv.at[hp, q], (b, h - 1, s)
        )

    def swap_slot(bb, q):
        return cot_all.at[pl.ds(q * rows, rows), pl.ds(pl.multiple_of(bb * tokens, tokens), tokens)]

    def swap(hp, q):
        return remote(
            line_slot(hp, q), swap_slot(b, q), swap_send.at[hp, q], swap_recv.at[b, q], (hp, h, s)
        )

    def swap_here(q):
        return pltpu.make_async_copy(line_slot(b, q), swap_slot(b, q), swap_local.at[q])

    def pass_on(hp, q):
        @pl.when(hp == b)
        def _():
            swap_here(q).start()

        @pl.when(hp != b)
        def _():
            swap(hp, q).start()

    far = n_batch // 2
    acts_moves = []

    def acts_move(bb, ss, device):
        index = len(acts_moves)
        move = remote(
            acts_slot(bb, ss), acts_slot(bb, ss), acts_send.at[index], acts_recv.at[bb, ss], device
        )
        move.start()
        acts_moves.append(move)

    def acts_wait(bb, ss):
        remote(acts_slot(bb, ss), acts_slot(bb, ss), acts_send.at[0], acts_recv.at[bb, ss], (b, h, s)).wait_recv()

    acts_move(b, s, (flip(b, far), h, s))
    acts_move(b, s, (b, h, 1 - s))
    for q in range(PIECES):
        @pl.when(h < n_line - 1)
        def _():
            up(h, q).start()

        @pl.when(h > 0)
        def _():
            down(h, q).start()

    near = [bits for bits in range(1, far)]
    for bits in near:
        acts_move(b, s, (flip(b, bits), h, s))
    for q in range(PIECES):
        pass_on(h, q)
    acts_wait(flip(b, far), s)
    acts_move(flip(b, far), s, (b, h, 1 - s))
    for bits in near:
        acts_move(flip(b, far), s, (flip(b, bits), h, s))
    weight_move = remote(weight_from(1 - s), weight_slot(s), weight_send, weight_recv, (b, h, 1 - s))
    weight_move.start()
    for place in (b, flip(b, far)):
        acts_wait(place, 1 - s)
        for bits in near:
            acts_move(place, 1 - s, (flip(b, bits), h, s))

    for distance in range(1, n_line):
        for q in range(PIECES):
            @pl.when(h >= distance)
            def _():
                hp = h - distance
                up(hp, q).wait_recv()

                @pl.when(h < n_line - 1)
                def _():
                    up(hp, q).start()

                pass_on(hp, q)

            @pl.when(h + distance < n_line)
            def _():
                hp = h + distance
                down(hp, q).wait_recv()

                @pl.when(h > 0)
                def _():
                    down(hp, q).start()

                pass_on(hp, q)

    for bits in near:
        for place in (flip(b, bits), flip(b, bits + far)):
            for ss in range(2):
                acts_wait(place, ss)
    own_weight.wait()
    weight_move.wait_recv()

    def first_tile(i, carry):
        at = pl.ds(pl.multiple_of(i * TILE, TILE), TILE)
        first_ref[at, :] = jnp.dot(
            acts_all[at, :], weight_all[...], preferred_element_type=jnp.float32
        ).astype(jnp.bfloat16)
        return carry

    lax.fori_loop(0, acts_all.shape[0] // TILE, first_tile, 0)

    for q in range(PIECES):
        swap_here(q).wait()
        for bits in range(1, n_batch):
            place = flip(b, bits)
            remote(
                swap_slot(place, q), swap_slot(place, q), swap_send.at[0, q], swap_recv.at[place, q], (b, h, s)
            ).wait_recv()

    def grad_tile(i, carry):
        at = pl.ds(pl.multiple_of(i * TILE, TILE), TILE)
        grad_ref[at, :] = jnp.dot(
            cot_all[at, :], acts_all[...], preferred_element_type=jnp.float32
        ).astype(jnp.bfloat16)
        return carry

    lax.fori_loop(0, outs // TILE, grad_tile, 0)

    for move in acts_moves:
        move.wait_send()
    weight_move.wait_send()
    for hp in range(n_line):
        for q in range(PIECES):
            @pl.when((hp <= h) & (h < n_line - 1))
            def _():
                up(hp, q).wait_send()

            @pl.when((hp >= h) & (h > 0))
            def _():
                down(hp, q).wait_send()

            @pl.when(hp != b)
            def _():
                swap(hp, q).wait_send()


def gather(activations, cotangent, weight, n_batch, n_line):
    tokens, feats = activations.shape
    outs = cotangent.shape[0]
    all_tokens, block = n_batch * tokens, 2 * feats
    vmem = pl.BlockSpec(memory_space=pltpu.VMEM)
    sem = pltpu.SemaphoreType.DMA
    bf = jnp.bfloat16
    return pl.pallas_call(
        functools.partial(gather_kernel, n_batch, n_line),
        out_shape=(
            jax.ShapeDtypeStruct((outs, block), bf),
            jax.ShapeDtypeStruct((all_tokens, block), bf),
            jax.ShapeDtypeStruct((block, outs), bf),
            jax.ShapeDtypeStruct((all_tokens, outs), bf),
        ),
        in_specs=[pl.BlockSpec(memory_space=pl.ANY)] * 3,
        out_specs=(vmem,) * 4,
        scratch_shapes=[
            pltpu.VMEM((n_line, outs, tokens), bf),
            pltpu.VMEM((outs, all_tokens), bf),
            sem((3,)),
            sem((2 * n_batch - 1,)),
            sem((n_batch, 2)),
            sem,
            sem,
            sem((2, n_line, PIECES)),
            sem((n_line, PIECES)),
            sem((n_line, PIECES)),
            sem((n_batch, PIECES)),
            sem((PIECES,)),
        ],
        compiler_params=pltpu.CompilerParams(
            collective_id=0, has_side_effects=True, vmem_limit_bytes=VMEM_LIMIT
        ),
        name="gather",
    )(activations, cotangent, weight)


def tiles(count, step):
    lax.fori_loop(0, count, lambda i, carry: (step(i), carry)[1], 0)


def rows_at(i, size=TILE):
    return pl.ds(pl.multiple_of(i * size, size), size)


def dot(left, right):
    return jnp.dot(left, right, preferred_element_type=jnp.float32)


def update_statistics(old, left, right, own, sent, worst, s):
    half = old.shape[0] // 2
    worst[...] = jnp.zeros_like(worst)

    def step(i):
        at = rows_at(i)
        new = STAT_DECAY * old[at, :] + (1.0 - STAT_DECAY) / BLOCK * dot(left[at, :], right[...])
        old[at, :] = new
        worst[...] = jnp.maximum(
            worst[...], jnp.max(jnp.sum(jnp.abs(new), axis=1, keepdims=True), axis=0, keepdims=True)
        )

    tiles(old.shape[0] // TILE, step)

    def split(i):
        here = rows_at(i)
        first = pl.multiple_of(s * half + i * TILE, TILE)
        other = pl.multiple_of((1 - s) * half + i * TILE, TILE)
        own[here, :] = old[pl.ds(first, TILE), :]
        sent[here, :] = old[pl.ds(other, TILE), :].astype(jnp.bfloat16)

    tiles(half // TILE, split)


def series(stat, worst, step_one, step_two, step_three, tail):
    size = stat.shape[0]
    scaled = 2.5 / (worst[...] + EPSILON)

    def first(i):
        at = rows_at(i)
        row = lax.broadcasted_iota(jnp.int32, (TILE, size), 0) + i * TILE
        col = lax.broadcasted_iota(jnp.int32, (TILE, size), 1)
        diagonal = jnp.where(row == col, 0.25, 0.0)
        step_one[at, :] = (diagonal - (0.25 * scaled) * stat[at, :]).astype(jnp.bfloat16)

    tiles(size // TILE, first)

    def second(i):
        at = rows_at(i)
        two = dot(step_one[at, :], step_one[...])
        two_low = two.astype(jnp.bfloat16)
        three = dot(two_low, step_one[...])
        step_two[at, :] = two_low
        step_three[at, :] = three.astype(jnp.bfloat16)
        tail[at, :] = (8.75 * step_one[at, :].astype(jnp.float32) + 4.75 * two + three).astype(jnp.bfloat16)

    tiles(size // TILE, second)
    return jnp.sqrt(jnp.sqrt(scaled))


def root_rows(at, step_one, step_two, step_three, tail):
    f32 = jnp.float32
    return (
        step_one[at, :].astype(f32)
        + 2.5 * step_two[at, :].astype(f32)
        + 7.5 * step_three[at, :].astype(f32)
        + dot(step_three[at, :], tail[...])
    ).astype(jnp.bfloat16)


def block_kernel(
    grad_ref,
    acts_ref,
    weight_ref,
    left_ref,
    right_ref,
    left_own,
    left_sent,
    right_own,
    right_sent,
    direction_own,
    direction_sent,
    second_ref,
    left,
    right,
    turned,
    one,
    two,
    three,
    tail,
    root,
    update,
    worst,
    squares,
    sems,
):
    s = lax.axis_index("solver")
    left_in = pltpu.make_async_copy(left_ref.at[0, s], left, sems.at[0])
    right_in = pltpu.make_async_copy(right_ref.at[0, s], right, sems.at[1])
    left_in.start()
    right_in.start()

    def turn(i):
        turned[:, rows_at(i)] = grad_ref[rows_at(i), :].T

    for i in range(grad_ref.shape[0] // TILE):
        turn(i)

    right_in.wait()
    update_statistics(right, grad_ref, turned, right_own, right_sent, worst, s)
    scale_right = series(right, worst, one, two, three, tail)

    def right_root(i):
        root[rows_at(i), :] = root_rows(rows_at(i), one, two, three, tail)

    tiles(BLOCK // TILE, right_root)

    left_in.wait()
    update_statistics(left, turned, grad_ref, left_own, left_sent, worst, s)
    scale = series(left, worst, one, two, three, tail) * scale_right
    squares[...] = jnp.zeros_like(squares)

    def apply(i):
        at = rows_at(i)
        left_rows = root_rows(at, one, two, three, tail)
        mixed = turned[at, :].astype(jnp.float32) + dot(left_rows, turned[...])
        value = mixed + dot(mixed.astype(jnp.bfloat16), root[...])
        update[at, :] = value
        squares[...] += jnp.sum(jnp.sum(value * value, axis=1, keepdims=True), axis=0, keepdims=True)

    tiles(BLOCK // TILE, apply)
    scaled = scale / jnp.sqrt(scale * scale * squares[...] / (BLOCK * BLOCK) + EPSILON)
    half = BLOCK // 2

    def finish(i):
        at = rows_at(i)
        root[at, :] = (
            weight_ref[at, :].astype(jnp.float32) - LEARN_RATE * (scaled * update[at, :])
        ).astype(jnp.bfloat16)

    tiles(BLOCK // TILE, finish)

    def forward(i):
        at = rows_at(i)
        second_ref[at, :] = dot(acts_ref[at, :], root[...]).astype(jnp.bfloat16)

    tiles(acts_ref.shape[0] // TILE, forward)

    def split(i):
        here = rows_at(i)
        first = pl.multiple_of(s * half + i * TILE, TILE)
        other = pl.multiple_of((1 - s) * half + i * TILE, TILE)
        direction_own[here, :] = scaled * update[pl.ds(first, TILE), :]
        direction_sent[here, :] = (scaled * update[pl.ds(other, TILE), :]).astype(jnp.bfloat16)

    tiles(half // TILE, split)


def block_step(grad, acts, weight, left_old, right_old):
    f32, bf = jnp.float32, jnp.bfloat16
    half = BLOCK // 2
    vmem = pl.BlockSpec(memory_space=pltpu.VMEM)
    hbm = pl.BlockSpec(memory_space=pl.ANY)
    own, sent = jax.ShapeDtypeStruct((half, BLOCK), f32), jax.ShapeDtypeStruct((half, BLOCK), bf)
    low = pltpu.VMEM((BLOCK, BLOCK), bf)
    wide = pltpu.VMEM((BLOCK, BLOCK), f32)
    return pl.pallas_call(
        block_kernel,
        out_shape=(own, sent, own, sent, own, sent, jax.ShapeDtypeStruct(acts.shape, bf)),
        in_specs=[vmem] * 3 + [hbm] * 2,
        out_specs=(vmem,) * 7,
        scratch_shapes=[
            wide,
            wide,
            low,
            low,
            low,
            low,
            low,
            low,
            wide,
            pltpu.VMEM((1, 1), f32),
            pltpu.VMEM((1, 1), f32),
            pltpu.SemaphoreType.DMA((2,)),
        ],
        compiler_params=pltpu.CompilerParams(vmem_limit_bytes=VMEM_LIMIT),
        name="block_step",
    )(grad, acts, weight, left_old, right_old)


def scatter_kernel(n_batch, n_line, *refs):
    partials, sent = refs[0:2], refs[2:5]
    outs, got = refs[5:7], refs[7:10]
    inbox, from_above, from_below = refs[10:13]
    side_send, side_recv, local, swap_send, swap_recv, line_send, line_recv = refs[13:]
    b, h, s = position()
    tokens = outs[0].shape[0]
    rows = tokens // PIECES

    line_barrier(n_batch, n_line)

    def piece(p, bb, q):
        return inbox.at[p, bb, pl.ds(q * rows, rows)]

    def outgoing(p, bb, q):
        return partials[p].at[pl.ds(pl.multiple_of(bb * tokens + q * rows, rows), rows)]

    def own(p, q):
        return pltpu.make_async_copy(outgoing(p, b, q), piece(p, b, q), local.at[p, q])

    def swap(p, bits, q):
        to = flip(b, bits)
        return remote(
            outgoing(p, to, q), piece(p, b, q), swap_send.at[p, bits, q], swap_recv.at[p, bits, q], (to, h, s)
        )

    def down(p, bb, q):
        at = pl.ds(q * rows, rows)
        return (from_above.at[p, bb, at], line_send.at[p, bb, q], line_recv.at[p, 0, bb, q], (b, h - 1, s))

    def up(p, bb, q):
        at = pl.ds(q * rows, rows)
        return (from_below.at[p, bb, at], line_send.at[p, bb, q], line_recv.at[p, 1, bb, q], (b, h + 1, s))

    def line(how, p, bb, q, first):
        slot, send, recv, device = how(p, bb, q)
        return remote(piece(p, bb, q) if first else slot, slot, send, recv, device)

    def add(slot, p, bb, q):
        slot[...] = (slot[...].astype(jnp.float32) + piece(p, bb, q)[...].astype(jnp.float32)).astype(slot.dtype)

    side = [
        remote(sent[i], got[i], side_send.at[i], side_recv.at[i], (b, h, 1 - s)) for i in range(len(sent))
    ]
    order = [n_batch // 2 + bits for bits in range(n_batch // 2)] + list(range(1, n_batch // 2))
    for p in range(len(partials)):
        for q in range(PIECES):
            own(p, q).start()
        for bits in order:
            for q in range(PIECES):
                swap(p, bits, q).start()
        if p == 0:
            for move in side:
                move.start()

    for p in range(len(partials)):
        for bits in range(n_batch):
            bb = flip(b, bits)
            for q in range(PIECES):
                if bits == 0:
                    own(p, q).wait()
                else:
                    swap(p, bits, q).wait_recv()

                def forward(how, first):
                    @pl.when(first)
                    def _():
                        line(how, p, bb, q, True).start()

                    @pl.when(jnp.logical_not(first))
                    def _():
                        line(how, p, bb, q, False).wait_recv()
                        add(how(p, bb, q)[0], p, bb, q)
                        line(how, p, bb, q, False).start()

                @pl.when(bb < h)
                def _():
                    forward(down, h == n_line - 1)

                @pl.when(bb > h)
                def _():
                    forward(up, h == 0)

        for q in range(PIECES):
            at = pl.ds(q * rows, rows)
            outs[p][at, :] = piece(p, h, q)[...]

            @pl.when(h < n_line - 1)
            def _():
                line(down, p, h, q, False).wait_recv()
                outs[p][at, :] = (
                    outs[p][at, :].astype(jnp.float32) + from_above[p, h, at].astype(jnp.float32)
                ).astype(outs[p].dtype)

            @pl.when(h > 0)
            def _():
                line(up, p, h, q, False).wait_recv()
                outs[p][at, :] = (
                    outs[p][at, :].astype(jnp.float32) + from_below[p, h, at].astype(jnp.float32)
                ).astype(outs[p].dtype)

    for p in range(len(partials)):
        for q in range(PIECES):
            for bits in range(1, n_batch):
                swap(p, bits, q).wait_send()
            for bb in range(n_line):
                @pl.when(h > bb)
                def _():
                    line(down, p, bb, q, False).wait_send()

                @pl.when(h < bb)
                def _():
                    line(up, p, bb, q, False).wait_send()

    for move in side:
        move.wait()


def scatter(partials, sent, n_batch, n_line):
    all_tokens, width = partials[0].shape
    tokens = all_tokens // n_batch
    vmem = pl.BlockSpec(memory_space=pltpu.VMEM)
    hbm = pl.BlockSpec(memory_space=pl.ANY)
    sem = pltpu.SemaphoreType.DMA
    bf = jnp.bfloat16
    many = len(partials)
    return pl.pallas_call(
        functools.partial(scatter_kernel, n_batch, n_line),
        out_shape=tuple(jax.ShapeDtypeStruct((tokens, width), bf) for _ in partials)
        + tuple(jax.ShapeDtypeStruct(part.shape, part.dtype) for part in sent),
        in_specs=[hbm] * (many + len(sent)),
        out_specs=(vmem,) * many + (hbm,) * len(sent),
        scratch_shapes=[
            pltpu.VMEM((many, n_batch, tokens, width), bf),
            pltpu.VMEM((many, n_line, tokens, width), bf),
            pltpu.VMEM((many, n_line, tokens, width), bf),
            sem((len(sent),)),
            sem((len(sent),)),
            sem((many, PIECES)),
            sem((many, n_batch, PIECES)),
            sem((many, n_batch, PIECES)),
            sem((many, n_line, PIECES)),
            sem((many, 2, n_line, PIECES)),
        ],
        compiler_params=pltpu.CompilerParams(
            collective_id=1, has_side_effects=True, vmem_limit_bytes=VMEM_LIMIT
        ),
        name="scatter",
    )(*partials, *sent)


def owned_body(activations, cotangent, weight, left_old, right_old, *, n_batch, n_line):
    s = lax.axis_index("solver")
    grad, acts, block_weight, first_partial = gather(activations, cotangent, weight, n_batch, n_line)
    left_own, left_sent, right_own, right_sent, direction_own, direction_sent, second_partial = block_step(
        grad, acts, block_weight, left_old, right_old
    )
    first, second, left_got, right_got, direction_got = scatter(
        (first_partial, second_partial), (left_sent, right_sent, direction_sent), n_batch, n_line
    )

    def joined(own, got, axis):
        got = got.astype(jnp.float32)
        return jnp.where(s == 0, jnp.stack([own, got], axis), jnp.stack([got, own], axis))

    new_left = joined(left_own, left_got, 0)[None]
    new_right = joined(right_own, right_got, 0)[None]
    direction = joined(direction_own, direction_got, 1).reshape(direction_own.shape[0], -1)
    return (first.T, new_left, new_right, direction, second.T)


def solution(mesh):
    in_specs = (
        P("batch", ("hidden", "solver")),
        P(("hidden", "solver"), "batch"),
        P(("hidden", "solver"), "batch"),
        P("hidden", "batch", None, None),
        P("hidden", "batch", None, None),
    )
    out_specs = (
        P(("hidden", "solver"), "batch"),
        P("hidden", "batch", "solver", None),
        P("hidden", "batch", "solver", None),
        P(("hidden", "solver"), "batch"),
        P(("hidden", "solver"), "batch"),
    )
    n_batch = mesh.shape["batch"]
    n_feat = mesh.shape["hidden"] * mesh.shape["solver"]

    n_line = mesh.shape["hidden"]
    n_solver = mesh.shape["solver"]

    def owned(activations, cotangent, weight, left_old, right_old):
        blocks = left_old.shape[1]
        even = n_line == n_batch and n_batch & (n_batch - 1) == 0 and n_batch > 2
        return even and n_solver == 2 and blocks == n_solver and cotangent.shape[0] == BLOCK

    def step(activations, cotangent, weight, left_old, right_old):
        args = (activations, cotangent, weight, left_old, right_old)
        if owned(*args):
            return owned_body(*args, n_batch=n_batch, n_line=n_line)
        return body(
            activations,
            cotangent,
            weight,
            left_old,
            right_old,
            n_batch=n_batch,
            n_solver=mesh.shape["solver"],
            n_feat=n_feat,
        )

    return jax.shard_map(step, mesh=mesh, in_specs=in_specs, out_specs=out_specs, check_vma=False)
```

```python
import functools

import jax
import jax.numpy as jnp
from jax import lax
from jax.experimental import pallas as pl
from jax.experimental.pallas import tpu as pltpu
from jax.sharding import PartitionSpec as P

BLOCK = 1024


STAT_DECAY = 0.8
LEARN_RATE = 0.005
EPSILON = 1e-06

ALL = ("batch", "hidden", "solver")
FEATURES = ("hidden", "solver")


def product(left_mat, right_mat):
    return jnp.einsum("bij,bjk->bik", left_mat, right_mat, preferred_element_type=jnp.float32)


def prepare(factor):
    identity = jnp.eye(BLOCK, dtype=jnp.float32)
    scaled = 2.5 / (jnp.max(jnp.sum(jnp.abs(factor), axis=2), axis=1) + EPSILON)
    moment = scaled[:, None, None] * factor
    newton_step = (5.0 * identity - moment) * 0.25
    return (scaled, moment.astype(jnp.bfloat16), newton_step.astype(jnp.bfloat16))


def apply_root(start, moment, step):
    power = start
    for _ in range(4):
        power = product(power.astype(jnp.bfloat16), step)
    power = product(power.astype(jnp.bfloat16), moment)
    return (5.0 * start.astype(jnp.float32) - power) * 0.25


def body(activations, cotangent, weight, left_old, right_old, *, n_batch, n_solver, n_feat):
    rows_here = weight.shape[0]
    nblocks = weight.shape[1] // BLOCK
    per_batch = n_feat // n_batch
    out_rows = weight.shape[1] // per_batch
    tokens = activations.shape[0]
    to_owner = [
        (b * n_feat + c * n_batch + t, t * n_feat + b * per_batch + c)
        for b in range(n_batch)
        for c in range(per_batch)
        for t in range(n_batch)
    ]
    from_owner = [(target, source) for source, target in to_owner]

    def partial_forward(weight_here):
        split = weight_here.reshape(rows_here, per_batch, out_rows)
        out = jnp.einsum("fco,btf->cbot", split, acts_all, preferred_element_type=jnp.float32)
        return out.astype(jnp.bfloat16).reshape(n_feat * out_rows, tokens)

    def reduce_forward(partial):
        return lax.psum_scatter(partial, FEATURES, scatter_dimension=0, tiled=True)

    acts_all = lax.all_gather(activations, "batch", axis=0, tiled=False)
    here = lax.axis_index("solver")
    acts_block = jnp.zeros((n_batch, tokens, n_solver * rows_here), acts_all.dtype)
    for shift in range(n_solver):
        part = acts_all
        if shift > 0:
            pairs = [(at, (at + shift) % n_solver) for at in range(n_solver)]
            part = lax.ppermute(acts_all, "solver", pairs)
        first_col = lax.rem(here + n_solver - shift, n_solver) * rows_here
        acts_block = lax.dynamic_update_slice_in_dim(acts_block, part, first_col, 2)
    cot_moved = lax.ppermute(cotangent, ALL, from_owner)
    cot_all = lax.all_gather(cot_moved, FEATURES, axis=0, tiled=False)
    cot_all = cot_all.reshape(per_batch, n_batch, out_rows, tokens)
    first_partial = partial_forward(weight)
    first_partial, cot_all = lax.optimization_barrier((first_partial, cot_all))
    first_sum = reduce_forward(first_partial)
    grad_full = jnp.einsum("cbot,btf->cof", cot_all, acts_block, preferred_element_type=jnp.float32)
    grad_full = grad_full.astype(jnp.bfloat16).reshape(nblocks, BLOCK, BLOCK)
    gram_left = jnp.einsum("bnm,bnk->bmk", grad_full, grad_full, preferred_element_type=jnp.float32)
    gram_right = jnp.einsum(
        "bnm,bkm->bnk", grad_full, grad_full, preferred_element_type=jnp.float32
    )
    left_all = STAT_DECAY * left_old[0] + (1.0 - STAT_DECAY) / BLOCK * gram_left
    right_all = STAT_DECAY * right_old[0] + (1.0 - STAT_DECAY) / BLOCK * gram_right
    first_row = lax.axis_index("solver") * rows_here
    new_left = lax.dynamic_slice_in_dim(left_all, first_row, rows_here, 1)[None]
    new_right = lax.dynamic_slice_in_dim(right_all, first_row, rows_here, 1)[None]
    scale_left, moment_left, step_left = prepare(left_all)
    own_rows = lax.dynamic_slice_in_dim(step_left, first_row, rows_here, 1)
    root_rows = apply_root(own_rows, moment_left, step_left)
    mixed_rows = jnp.einsum(
        "brm,bnm->brn",
        root_rows.astype(jnp.bfloat16),
        grad_full,
        preferred_element_type=jnp.float32,
    )
    scale_right, moment_right, step_right = prepare(right_all)
    turned = product(mixed_rows.astype(jnp.bfloat16), step_right)
    scale_both = (scale_left**0.25) * (scale_right**0.25)
    update = scale_both[:, None, None] * apply_root(turned, moment_right, step_right)
    update, first_sum = lax.optimization_barrier((update, first_sum))
    first_out = lax.ppermute(first_sum, ALL, to_owner)
    squares = lax.psum(jnp.sum(update * update, axis=(1, 2)), "solver")
    spread = jnp.sqrt(squares / (BLOCK * BLOCK) + EPSILON)
    scaled_update = update / spread[:, None, None]
    direction = jnp.transpose(scaled_update, (1, 0, 2)).reshape(rows_here, nblocks * BLOCK)
    new_weight = (weight.astype(jnp.float32) - LEARN_RATE * direction).astype(jnp.bfloat16)
    second_sum = reduce_forward(partial_forward(new_weight))
    second_sum, new_left, new_right = lax.optimization_barrier((second_sum, new_left, new_right))
    second_out = lax.ppermute(second_sum, ALL, to_owner)
    return (first_out, new_left, new_right, direction, second_out)


MESH = pl.DeviceIdType.MESH
VMEM_LIMIT = 62 * 1024 * 1024
PIECES = 4
TILE = 256


def remote(src, dst, send_sem, recv_sem, device):
    return pltpu.make_async_remote_copy(
        src_ref=src,
        dst_ref=dst,
        send_sem=send_sem,
        recv_sem=recv_sem,
        device_id=device,
        device_id_type=MESH,
    )


def position():
    return lax.axis_index("batch"), lax.axis_index("hidden"), lax.axis_index("solver")


def flip(index, bits):
    bit = 1
    while bit <= bits:
        if bits & bit:
            index = index + bit * (1 - 2 * ((index // bit) % 2))
        bit *= 2
    return index


def line_barrier(n_batch, n_line):
    b, h, s = position()
    barrier = pltpu.get_barrier_semaphore()
    for bits in range(1, n_batch):
        pl.semaphore_signal(barrier, inc=1, device_id=(flip(b, bits), h, s), device_id_type=MESH)
    pl.semaphore_signal(barrier, inc=1, device_id=(b, h, 1 - s), device_id_type=MESH)

    @pl.when(h > 0)
    def _():
        pl.semaphore_signal(barrier, inc=1, device_id=(b, h - 1, s), device_id_type=MESH)

    @pl.when(h < n_line - 1)
    def _():
        pl.semaphore_signal(barrier, inc=1, device_id=(b, h + 1, s), device_id_type=MESH)

    ends = (h == 0).astype(jnp.int32) + (h == n_line - 1).astype(jnp.int32)
    pl.semaphore_wait(barrier, n_batch + 2 - ends)


def tiles(count, step):
    lax.fori_loop(0, count, lambda i, carry: (step(i), carry)[1], 0)


def rows_at(i, size=TILE):
    return pl.ds(pl.multiple_of(i * size, size), size)


def dot(left, right):
    return jnp.dot(left, right, preferred_element_type=jnp.float32)


def update_statistics(old, left, right, own, sent, worst, s):
    half = old.shape[0] // 2
    worst[...] = jnp.zeros_like(worst)

    def step(i):
        at = rows_at(i)
        new = STAT_DECAY * old[at, :] + (1.0 - STAT_DECAY) / BLOCK * dot(left[at, :], right[...])
        old[at, :] = new
        worst[...] = jnp.maximum(
            worst[...], jnp.max(jnp.sum(jnp.abs(new), axis=1, keepdims=True), axis=0, keepdims=True)
        )

    tiles(old.shape[0] // TILE, step)

    def split(i):
        here = rows_at(i)
        first = pl.multiple_of(s * half + i * TILE, TILE)
        other = pl.multiple_of((1 - s) * half + i * TILE, TILE)
        own[here, :] = old[pl.ds(first, TILE), :].astype(own.dtype)
        sent[here, :] = old[pl.ds(other, TILE), :].astype(sent.dtype)

    tiles(half // TILE, split)


def series(stat, worst, step_one, step_two, step_three, tail, beside):
    size = stat.shape[0]
    scaled = 2.5 / (worst[...] + EPSILON)

    def first(i):
        at = rows_at(i)
        row = lax.broadcasted_iota(jnp.int32, (TILE, size), 0) + i * TILE
        col = lax.broadcasted_iota(jnp.int32, (TILE, size), 1)
        diagonal = jnp.where(row == col, 0.25, 0.0)
        step_one[at, :] = (diagonal - (0.25 * scaled) * stat[at, :]).astype(jnp.bfloat16)

    tiles(size // TILE, first)

    def second(i):
        at = rows_at(i)
        two = dot(step_one[at, :], step_one[...])
        two_low = two.astype(jnp.bfloat16)
        three = dot(two_low, step_one[...])
        step_two[at, :] = two_low
        step_three[at, :] = three.astype(jnp.bfloat16)
        tail[at, :] = (8.75 * step_one[at, :].astype(jnp.float32) + 4.75 * two + three).astype(jnp.bfloat16)
        beside(i)

    tiles(size // TILE, second)
    return jnp.sqrt(jnp.sqrt(scaled))


def root_rows(at, step_one, step_two, step_three, tail):
    f32 = jnp.float32
    return (
        step_one[at, :].astype(f32)
        + 2.5 * step_two[at, :].astype(f32)
        + 7.5 * step_three[at, :].astype(f32)
        + dot(step_three[at, :], tail[...])
    ).astype(jnp.bfloat16)


class Reduction:
    def __init__(self, n_batch, n_line, partial, out, inbox, from_above, from_below, sems):
        self.n_batch, self.n_line = n_batch, n_line
        self.partial, self.out, self.inbox = partial, out, inbox
        self.from_above, self.from_below = from_above, from_below
        self.local, self.swap_send, self.swap_recv, self.line_send, self.line_recv = sems
        self.b, self.h, self.s = position()
        self.tokens = out.shape[0]
        self.rows = self.tokens // PIECES

    def at(self, q):
        return pl.ds(pl.multiple_of(q * self.rows, self.rows), self.rows)

    def piece(self, bb, q):
        return self.inbox.at[bb, self.at(q)]

    def outgoing(self, bb, q):
        return self.partial.at[pl.ds(pl.multiple_of(bb * self.tokens + q * self.rows, self.rows), self.rows)]

    def own(self, q):
        return pltpu.make_async_copy(self.outgoing(self.b, q), self.piece(self.b, q), self.local.at[q])

    def swap(self, bits, q):
        to = flip(self.b, bits)
        return remote(
            self.outgoing(to, q),
            self.piece(self.b, q),
            self.swap_send.at[bits, q],
            self.swap_recv.at[bits, q],
            (to, self.h, self.s),
        )

    def down_slot(self, bb, q):
        return self.from_above.at[bb, self.at(q)]

    def up_slot(self, bb, q):
        return self.from_below.at[bb, self.at(q)]

    def down(self, bb, q, source):
        return remote(
            source,
            self.down_slot(bb, q),
            self.line_send.at[bb, q],
            self.line_recv.at[0, bb, q],
            (self.b, self.h - 1, self.s),
        )

    def up(self, bb, q, source):
        return remote(
            source,
            self.up_slot(bb, q),
            self.line_send.at[bb, q],
            self.line_recv.at[1, bb, q],
            (self.b, self.h + 1, self.s),
        )

    def start(self):
        half = self.n_batch // 2
        for q in range(PIECES):
            self.own(q).start()
        for bits in [half + low for low in range(half)] + list(range(1, half)):
            for q in range(PIECES):
                self.swap(bits, q).start()

    def arrive(self, bits, q):
        if bits == 0:
            self.own(q).wait()
        else:
            self.swap(bits, q).wait_recv()

    def open(self, bits, q):
        bb = flip(self.b, bits)

        @pl.when((bb < self.h) & (self.h == self.n_line - 1))
        def _():
            self.arrive(bits, q)
            self.down(bb, q, self.piece(bb, q)).start()

        @pl.when((bb > self.h) & (self.h == 0))
        def _():
            self.arrive(bits, q)
            self.up(bb, q, self.piece(bb, q)).start()

    def relay(self, bits, q):
        bb, h = flip(self.b, bits), self.h

        @pl.when(bb == h)
        def _():
            self.arrive(bits, q)

        def add(slot):
            slot[...] = (
                slot[...].astype(jnp.float32) + self.piece(bb, q)[...].astype(jnp.float32)
            ).astype(slot.dtype)

        @pl.when((bb < h) & (h < self.n_line - 1))
        def _():
            self.arrive(bits, q)
            slot = self.down_slot(bb, q)
            move = self.down(bb, q, slot)
            move.wait_recv()
            add(slot)
            move.start()

        @pl.when((bb > h) & (h > 0))
        def _():
            self.arrive(bits, q)
            slot = self.up_slot(bb, q)
            move = self.up(bb, q, slot)
            move.wait_recv()
            add(slot)
            move.start()

    def close(self, q):
        h, out, at = self.h, self.out, self.at(q)
        out[at, :] = self.piece(h, q)[...]

        @pl.when(h < self.n_line - 1)
        def _():
            slot = self.down_slot(h, q)
            self.down(h, q, slot).wait_recv()
            out[at, :] = (out[at, :].astype(jnp.float32) + slot[...].astype(jnp.float32)).astype(out.dtype)

        @pl.when(h > 0)
        def _():
            slot = self.up_slot(h, q)
            self.up(h, q, slot).wait_recv()
            out[at, :] = (out[at, :].astype(jnp.float32) + slot[...].astype(jnp.float32)).astype(out.dtype)

    def sent(self, q):
        for bits in range(1, self.n_batch):
            self.swap(bits, q).wait_send()
        for bb in range(self.n_line):
            @pl.when(self.h > bb)
            def _():
                self.down(bb, q, self.down_slot(bb, q)).wait_send()

            @pl.when(self.h < bb)
            def _():
                self.up(bb, q, self.up_slot(bb, q)).wait_send()


def step_kernel(n_batch, n_line, *refs):
    acts_ref, cot_ref, weight_ref, left_ref, right_ref = refs[0:5]
    first_out, second_out = refs[5:7]
    own_out, got_out = refs[7:10], refs[10:13]
    acts_all, weight_all, cot_line, cot_all, grad, turned = refs[13:19]
    left, right, one, two, three, tail, root = refs[19:26]
    partials = refs[26:28]
    inbox, from_above, from_below, own_rows, sent_rows, worst, squares = refs[28:35]
    local_sem, acts_send, acts_recv, weight_send, weight_recv = refs[35:40]
    line_send, line_recv, swap_send, swap_recv, swap_local = refs[40:45]
    side_send, side_recv, own_sem = refs[45:48]
    sums = refs[48:53]
    b, h, s = position()
    tokens, feats = acts_ref.shape
    outs = cot_ref.shape[0]
    rows = outs // PIECES
    reductions = [
        Reduction(
            n_batch,
            n_line,
            partials[p],
            (first_out, second_out)[p],
            inbox.at[p],
            from_above.at[p],
            from_below.at[p],
            [sem.at[p] for sem in sums],
        )
        for p in range(2)
    ]

    def acts_slot(bb, ss):
        return acts_all.at[
            pl.ds(pl.multiple_of(bb * tokens, tokens), tokens),
            pl.ds(pl.multiple_of(ss * feats, feats), feats),
        ]

    def weight_from(ss):
        return weight_ref.at[:, pl.ds(pl.multiple_of(ss * outs, outs), outs)]

    def weight_slot(ss):
        return weight_all.at[pl.ds(pl.multiple_of(ss * feats, feats), feats), :]

    own_cot = pltpu.make_async_copy(cot_ref, cot_line.at[h], local_sem.at[0])
    own_acts = pltpu.make_async_copy(acts_ref, acts_slot(b, s), local_sem.at[1])
    own_weight = pltpu.make_async_copy(weight_from(s), weight_slot(s), local_sem.at[2])
    left_in = pltpu.make_async_copy(left_ref.at[0, s], left, local_sem.at[3])
    right_in = pltpu.make_async_copy(right_ref.at[0, s], right, local_sem.at[4])
    own_cot.start()
    own_acts.start()
    line_barrier(n_batch, n_line)
    own_weight.start()
    right_in.start()
    left_in.start()
    own_acts.wait()
    own_cot.wait()

    def line_slot(hp, q):
        return cot_line.at[hp, pl.ds(q * rows, rows)]

    def up(hp, q):
        return remote(
            line_slot(hp, q), line_slot(hp, q), line_send.at[0, hp, q], line_recv.at[hp, q], (b, h + 1, s)
        )

    def down(hp, q):
        return remote(
            line_slot(hp, q), line_slot(hp, q), line_send.at[1, hp, q], line_recv.at[hp, q], (b, h - 1, s)
        )

    def swap_slot(bb, q):
        return cot_all.at[rows_at(q, rows), pl.ds(pl.multiple_of(bb * tokens, tokens), tokens)]

    def swap(hp, q):
        return remote(
            line_slot(hp, q), swap_slot(b, q), swap_send.at[hp, q], swap_recv.at[b, q], (hp, h, s)
        )

    def swap_here(q):
        return pltpu.make_async_copy(
            cot_line.at[b, rows_at(q, rows)], swap_slot(b, q), swap_local.at[q]
        )

    def pass_on(hp, q):
        @pl.when(hp == b)
        def _():
            swap_here(q).start()

        @pl.when(hp != b)
        def _():
            swap(hp, q).start()

    far = n_batch // 2
    acts_moves = []

    def acts_move(bb, ss, device):
        index = len(acts_moves)
        move = remote(
            acts_slot(bb, ss), acts_slot(bb, ss), acts_send.at[index], acts_recv.at[bb, ss], device
        )
        move.start()
        acts_moves.append(move)

    def acts_wait(bb, ss):
        remote(acts_slot(bb, ss), acts_slot(bb, ss), acts_send.at[0], acts_recv.at[bb, ss], (b, h, s)).wait_recv()

    acts_move(b, s, (flip(b, far), h, s))
    acts_move(b, s, (b, h, 1 - s))
    for q in range(PIECES):
        @pl.when(h < n_line - 1)
        def _():
            up(h, q).start()

        @pl.when(h > 0)
        def _():
            down(h, q).start()

    near = [bits for bits in range(1, far)]
    for bits in near:
        acts_move(b, s, (flip(b, bits), h, s))
    for q in range(PIECES):
        pass_on(h, q)
    acts_wait(flip(b, far), s)
    acts_move(flip(b, far), s, (b, h, 1 - s))
    for bits in near:
        acts_move(flip(b, far), s, (flip(b, bits), h, s))
    weight_move = remote(weight_from(1 - s), weight_slot(s), weight_send, weight_recv, (b, h, 1 - s))
    weight_move.start()
    for place in (b, flip(b, far)):
        acts_wait(place, 1 - s)
        for bits in near:
            acts_move(place, 1 - s, (flip(b, bits), h, s))

    for distance in range(1, n_line):
        for q in range(PIECES):
            @pl.when(h >= distance)
            def _():
                hp = h - distance
                up(hp, q).wait_recv()

                @pl.when(h < n_line - 1)
                def _():
                    up(hp, q).start()

                pass_on(hp, q)

            @pl.when(h + distance < n_line)
            def _():
                hp = h + distance
                down(hp, q).wait_recv()

                @pl.when(h > 0)
                def _():
                    down(hp, q).start()

                pass_on(hp, q)

    for bits in near:
        for place in (flip(b, bits), flip(b, bits + far)):
            for ss in range(2):
                acts_wait(place, ss)
    own_weight.wait()
    weight_move.wait_recv()

    def forward(partial, block_weight):
        def step(i):
            at = rows_at(i)
            partial[at, :] = dot(acts_all[at, :], block_weight[...]).astype(jnp.bfloat16)

        tiles(acts_all.shape[0] // TILE, step)

    forward(partials[0], weight_all)
    first, second = reductions
    first.start()

    def early(q):
        first.open(0, q)
        first.open(1, q)

    tiles(PIECES, early)

    def grad_rows(q):
        swap_here(q).wait()
        for bits in range(1, n_batch):
            place = flip(b, bits)
            remote(
                swap_slot(place, q), swap_slot(place, q), swap_send.at[0, q], swap_recv.at[place, q], (b, h, s)
            ).wait_recv()
        at = rows_at(q, rows)
        value = dot(cot_all[at, :], acts_all[...]).astype(jnp.bfloat16)
        grad[at, :] = value
        turned[:, at] = value.T

    tiles(PIECES, grad_rows)

    own_moves, side_moves = [], []

    def exchange(i):
        own = pltpu.make_async_copy(own_rows.at[i], own_out[i], own_sem.at[i])
        side = remote(sent_rows.at[i], got_out[i], side_send.at[i], side_recv.at[i], (b, h, 1 - s))
        own.start()
        side.start()
        own_moves.append(own)
        side_moves.append(side)

    right_in.wait()
    update_statistics(right, grad, turned, own_rows.at[1], sent_rows.at[1], worst, s)
    exchange(1)

    def beside_right(q):
        first.open(2, q)
        first.relay(0, q)

    scale_right = series(right, worst, one, two, three, tail, beside_right)

    def right_root(i):
        root[rows_at(i), :] = root_rows(rows_at(i), one, two, three, tail)

    tiles(BLOCK // TILE, right_root)

    left_in.wait()
    update_statistics(left, turned, grad, own_rows.at[0], sent_rows.at[0], worst, s)
    exchange(0)

    def beside_left(q):
        first.open(3, q)
        first.relay(1, q)

    scale = series(left, worst, one, two, three, tail, beside_left) * scale_right
    squares[...] = jnp.zeros_like(squares)
    update = left

    def apply(i):
        at = rows_at(i)
        left_rows = root_rows(at, one, two, three, tail)
        mixed = turned[at, :].astype(jnp.float32) + dot(left_rows, turned[...])
        value = mixed + dot(mixed.astype(jnp.bfloat16), root[...])
        update[at, :] = value
        squares[...] += jnp.sum(jnp.sum(value * value, axis=1, keepdims=True), axis=0, keepdims=True)
        first.relay(2, i)

    tiles(BLOCK // TILE, apply)
    scaled = scale / jnp.sqrt(scale * scale * squares[...] / (BLOCK * BLOCK) + EPSILON)
    half = BLOCK // 2

    def finish(i):
        at = rows_at(i)
        root[at, :] = (
            weight_all[at, :].astype(jnp.float32) - LEARN_RATE * (scaled * update[at, :])
        ).astype(jnp.bfloat16)

    tiles(BLOCK // TILE, finish)
    forward(partials[1], root)
    second.start()

    def split(i):
        here = rows_at(i)
        mine = pl.multiple_of(s * half + i * TILE, TILE)
        other = pl.multiple_of((1 - s) * half + i * TILE, TILE)
        own_rows[2, here, :] = (scaled * update[pl.ds(mine, TILE), :]).astype(jnp.bfloat16)
        sent_rows[2, here, :] = (scaled * update[pl.ds(other, TILE), :]).astype(jnp.bfloat16)

    tiles(half // TILE, split)
    exchange(2)

    tiles(PIECES, lambda q: first.relay(3, q))
    for bits in range(n_batch):
        def both(q):
            second.open(bits, q)
            second.relay(bits, q)

        tiles(PIECES, both)
    tiles(PIECES, first.close)
    tiles(PIECES, second.close)

    for move in acts_moves:
        move.wait_send()
    weight_move.wait_send()
    for hp in range(n_line):
        for q in range(PIECES):
            @pl.when((hp <= h) & (h < n_line - 1))
            def _():
                up(hp, q).wait_send()

            @pl.when((hp >= h) & (h > 0))
            def _():
                down(hp, q).wait_send()

            @pl.when(hp != b)
            def _():
                swap(hp, q).wait_send()
    for reduction in reductions:
        tiles(PIECES, reduction.sent)
    for move in own_moves:
        move.wait()
    for move in side_moves:
        move.wait()


def block_step(activations, cotangent, weight, left_old, right_old, n_batch, n_line):
    tokens, feats = activations.shape
    outs = cotangent.shape[0]
    all_tokens, half = n_batch * tokens, BLOCK // 2
    vmem = pl.BlockSpec(memory_space=pltpu.VMEM)
    hbm = pl.BlockSpec(memory_space=pl.ANY)
    sem = pltpu.SemaphoreType.DMA
    bf, f32 = jnp.bfloat16, jnp.float32
    out = jax.ShapeDtypeStruct((tokens, outs), bf)
    part = jax.ShapeDtypeStruct((half, BLOCK), bf)
    low, wide = pltpu.VMEM((BLOCK, BLOCK), bf), pltpu.VMEM((BLOCK, BLOCK), f32)
    partial = pltpu.VMEM((all_tokens, outs), bf)
    return pl.pallas_call(
        functools.partial(step_kernel, n_batch, n_line),
        out_shape=(out, out) + (part,) * 6,
        in_specs=[hbm] * 5,
        out_specs=(vmem,) * 2 + (hbm,) * 6,
        scratch_shapes=[
            pltpu.VMEM((all_tokens, BLOCK), bf),
            low,
            pltpu.VMEM((n_line, outs, tokens), bf),
            pltpu.VMEM((outs, all_tokens), bf),
            low,
            low,
            wide,
            wide,
            low,
            low,
            low,
            low,
            low,
            partial,
            partial,
            pltpu.VMEM((2, n_batch, tokens, outs), bf),
            pltpu.VMEM((2, n_line, tokens, outs), bf),
            pltpu.VMEM((2, n_line, tokens, outs), bf),
            pltpu.VMEM((3, half, BLOCK), bf),
            pltpu.VMEM((3, half, BLOCK), bf),
            pltpu.VMEM((1, 1), f32),
            pltpu.VMEM((1, 1), f32),
            sem((5,)),
            sem((2 * n_batch - 1,)),
            sem((n_batch, 2)),
            sem,
            sem,
            sem((2, n_line, PIECES)),
            sem((n_line, PIECES)),
            sem((n_line, PIECES)),
            sem((n_batch, PIECES)),
            sem((PIECES,)),
            sem((3,)),
            sem((3,)),
            sem((3,)),
            sem((2, PIECES)),
            sem((2, n_batch, PIECES)),
            sem((2, n_batch, PIECES)),
            sem((2, n_line, PIECES)),
            sem((2, 2, n_line, PIECES)),
        ],
        compiler_params=pltpu.CompilerParams(
            collective_id=0, has_side_effects=True, vmem_limit_bytes=VMEM_LIMIT
        ),
        name="block_step",
    )(activations, cotangent, weight, left_old, right_old)


ASSEMBLE_STEPS = 4


def assemble_kernel(
    left_own, right_own, direction_own, left_got, right_got, direction_got, first_in, second_in,
    first, left, right, direction, second,
):
    s = lax.axis_index("solver")
    width = direction_own.shape[1]
    for own, got, out in ((left_own, left_got, left), (right_own, right_got, right)):
        out[0, s] = own[...].astype(jnp.float32)
        out[0, 1 - s] = got[...].astype(jnp.float32)
    direction[:, pl.ds(pl.multiple_of(s * width, width), width)] = direction_own[...].astype(jnp.float32)
    direction[:, pl.ds(pl.multiple_of((1 - s) * width, width), width)] = direction_got[...].astype(jnp.float32)
    first[...] = first_in[...].T
    second[...] = second_in[...].T


def assemble(rows, first, second):
    half, width = rows[0].shape
    tokens, outs = first.shape
    step = half // ASSEMBLE_STEPS
    cols = outs // ASSEMBLE_STEPS
    f32 = jnp.float32
    part = pl.BlockSpec((step, width), lambda i: (i, 0))
    stat = pl.BlockSpec((1, 2, step, width), lambda i: (0, 0, i, 0))
    turned_in = pl.BlockSpec((tokens, cols), lambda i: (0, i))
    turned_out = pl.BlockSpec((cols, tokens), lambda i: (i, 0))
    return pl.pallas_call(
        assemble_kernel,
        grid=(ASSEMBLE_STEPS,),
        out_shape=(
            jax.ShapeDtypeStruct((outs, tokens), first.dtype),
            jax.ShapeDtypeStruct((1, 2, half, width), f32),
            jax.ShapeDtypeStruct((1, 2, half, width), f32),
            jax.ShapeDtypeStruct((half, 2 * width), f32),
            jax.ShapeDtypeStruct((outs, tokens), first.dtype),
        ),
        in_specs=[part] * 6 + [turned_in] * 2,
        out_specs=(turned_out, stat, stat, pl.BlockSpec((step, 2 * width), lambda i: (i, 0)), turned_out),
        compiler_params=pltpu.CompilerParams(vmem_limit_bytes=VMEM_LIMIT),
        name="assemble",
    )(*rows, first, second)


def owned_body(activations, cotangent, weight, left_old, right_old, *, n_batch, n_line):
    first, second, *rows = block_step(
        activations, cotangent, weight, left_old, right_old, n_batch, n_line
    )
    return assemble(rows, first, second)


def solution(mesh):
    in_specs = (
        P("batch", ("hidden", "solver")),
        P(("hidden", "solver"), "batch"),
        P(("hidden", "solver"), "batch"),
        P("hidden", "batch", None, None),
        P("hidden", "batch", None, None),
    )
    out_specs = (
        P(("hidden", "solver"), "batch"),
        P("hidden", "batch", "solver", None),
        P("hidden", "batch", "solver", None),
        P(("hidden", "solver"), "batch"),
        P(("hidden", "solver"), "batch"),
    )
    n_batch = mesh.shape["batch"]
    n_feat = mesh.shape["hidden"] * mesh.shape["solver"]

    n_line = mesh.shape["hidden"]
    n_solver = mesh.shape["solver"]

    def owned(activations, cotangent, weight, left_old, right_old):
        blocks = left_old.shape[1]
        even = n_line == n_batch == 2 * n_solver
        return even and n_solver == 2 and blocks == n_solver and cotangent.shape[0] == BLOCK

    def step(activations, cotangent, weight, left_old, right_old):
        args = (activations, cotangent, weight, left_old, right_old)
        if owned(*args):
            return owned_body(*args, n_batch=n_batch, n_line=n_line)
        return body(
            activations,
            cotangent,
            weight,
            left_old,
            right_old,
            n_batch=n_batch,
            n_solver=mesh.shape["solver"],
            n_feat=n_feat,
        )

    return jax.shard_map(step, mesh=mesh, in_specs=in_specs, out_specs=out_specs, check_vma=False)
```

```python
import functools

import jax
import jax.numpy as jnp
from jax import lax
from jax.experimental import pallas as pl
from jax.experimental.pallas import tpu as pltpu
from jax.sharding import PartitionSpec as P

BLOCK = 1024


STAT_DECAY = 0.8
LEARN_RATE = 0.005
EPSILON = 1e-06

ALL = ("batch", "hidden", "solver")
FEATURES = ("hidden", "solver")


def product(left_mat, right_mat):
    return jnp.einsum("bij,bjk->bik", left_mat, right_mat, preferred_element_type=jnp.float32)


def prepare(factor):
    identity = jnp.eye(BLOCK, dtype=jnp.float32)
    scaled = 2.5 / (jnp.max(jnp.sum(jnp.abs(factor), axis=2), axis=1) + EPSILON)
    moment = scaled[:, None, None] * factor
    newton_step = (5.0 * identity - moment) * 0.25
    return (scaled, moment.astype(jnp.bfloat16), newton_step.astype(jnp.bfloat16))


def apply_root(start, moment, step):
    power = start
    for _ in range(4):
        power = product(power.astype(jnp.bfloat16), step)
    power = product(power.astype(jnp.bfloat16), moment)
    return (5.0 * start.astype(jnp.float32) - power) * 0.25


def body(activations, cotangent, weight, left_old, right_old, *, n_batch, n_solver, n_feat):
    rows_here = weight.shape[0]
    nblocks = weight.shape[1] // BLOCK
    per_batch = n_feat // n_batch
    out_rows = weight.shape[1] // per_batch
    tokens = activations.shape[0]
    to_owner = [
        (b * n_feat + c * n_batch + t, t * n_feat + b * per_batch + c)
        for b in range(n_batch)
        for c in range(per_batch)
        for t in range(n_batch)
    ]
    from_owner = [(target, source) for source, target in to_owner]

    def partial_forward(weight_here):
        split = weight_here.reshape(rows_here, per_batch, out_rows)
        out = jnp.einsum("fco,btf->cbot", split, acts_all, preferred_element_type=jnp.float32)
        return out.astype(jnp.bfloat16).reshape(n_feat * out_rows, tokens)

    def reduce_forward(partial):
        return lax.psum_scatter(partial, FEATURES, scatter_dimension=0, tiled=True)

    acts_all = lax.all_gather(activations, "batch", axis=0, tiled=False)
    here = lax.axis_index("solver")
    acts_block = jnp.zeros((n_batch, tokens, n_solver * rows_here), acts_all.dtype)
    for shift in range(n_solver):
        part = acts_all
        if shift > 0:
            pairs = [(at, (at + shift) % n_solver) for at in range(n_solver)]
            part = lax.ppermute(acts_all, "solver", pairs)
        first_col = lax.rem(here + n_solver - shift, n_solver) * rows_here
        acts_block = lax.dynamic_update_slice_in_dim(acts_block, part, first_col, 2)
    cot_moved = lax.ppermute(cotangent, ALL, from_owner)
    cot_all = lax.all_gather(cot_moved, FEATURES, axis=0, tiled=False)
    cot_all = cot_all.reshape(per_batch, n_batch, out_rows, tokens)
    first_partial = partial_forward(weight)
    first_partial, cot_all = lax.optimization_barrier((first_partial, cot_all))
    first_sum = reduce_forward(first_partial)
    grad_full = jnp.einsum("cbot,btf->cof", cot_all, acts_block, preferred_element_type=jnp.float32)
    grad_full = grad_full.astype(jnp.bfloat16).reshape(nblocks, BLOCK, BLOCK)
    gram_left = jnp.einsum("bnm,bnk->bmk", grad_full, grad_full, preferred_element_type=jnp.float32)
    gram_right = jnp.einsum(
        "bnm,bkm->bnk", grad_full, grad_full, preferred_element_type=jnp.float32
    )
    left_all = STAT_DECAY * left_old[0] + (1.0 - STAT_DECAY) / BLOCK * gram_left
    right_all = STAT_DECAY * right_old[0] + (1.0 - STAT_DECAY) / BLOCK * gram_right
    first_row = lax.axis_index("solver") * rows_here
    new_left = lax.dynamic_slice_in_dim(left_all, first_row, rows_here, 1)[None]
    new_right = lax.dynamic_slice_in_dim(right_all, first_row, rows_here, 1)[None]
    scale_left, moment_left, step_left = prepare(left_all)
    own_rows = lax.dynamic_slice_in_dim(step_left, first_row, rows_here, 1)
    root_rows = apply_root(own_rows, moment_left, step_left)
    mixed_rows = jnp.einsum(
        "brm,bnm->brn",
        root_rows.astype(jnp.bfloat16),
        grad_full,
        preferred_element_type=jnp.float32,
    )
    scale_right, moment_right, step_right = prepare(right_all)
    turned = product(mixed_rows.astype(jnp.bfloat16), step_right)
    scale_both = (scale_left**0.25) * (scale_right**0.25)
    update = scale_both[:, None, None] * apply_root(turned, moment_right, step_right)
    update, first_sum = lax.optimization_barrier((update, first_sum))
    first_out = lax.ppermute(first_sum, ALL, to_owner)
    squares = lax.psum(jnp.sum(update * update, axis=(1, 2)), "solver")
    spread = jnp.sqrt(squares / (BLOCK * BLOCK) + EPSILON)
    scaled_update = update / spread[:, None, None]
    direction = jnp.transpose(scaled_update, (1, 0, 2)).reshape(rows_here, nblocks * BLOCK)
    new_weight = (weight.astype(jnp.float32) - LEARN_RATE * direction).astype(jnp.bfloat16)
    second_sum = reduce_forward(partial_forward(new_weight))
    second_sum, new_left, new_right = lax.optimization_barrier((second_sum, new_left, new_right))
    second_out = lax.ppermute(second_sum, ALL, to_owner)
    return (first_out, new_left, new_right, direction, second_out)


MESH = pl.DeviceIdType.MESH
VMEM_LIMIT = 62 * 1024 * 1024
PIECES = 4
TILE = 512


def remote(src, dst, send_sem, recv_sem, device):
    return pltpu.make_async_remote_copy(
        src_ref=src,
        dst_ref=dst,
        send_sem=send_sem,
        recv_sem=recv_sem,
        device_id=device,
        device_id_type=MESH,
    )


def position():
    return lax.axis_index("batch"), lax.axis_index("hidden"), lax.axis_index("solver")


def flip(index, bits):
    bit = 1
    while bit <= bits:
        if bits & bit:
            index = index + bit * (1 - 2 * ((index // bit) % 2))
        bit *= 2
    return index


def line_barrier(n_batch, n_line):
    b, h, s = position()
    barrier = pltpu.get_barrier_semaphore()
    for bits in range(1, n_batch):
        pl.semaphore_signal(barrier, inc=1, device_id=(flip(b, bits), h, s), device_id_type=MESH)
    pl.semaphore_signal(barrier, inc=1, device_id=(b, h, 1 - s), device_id_type=MESH)

    @pl.when(h > 0)
    def _():
        pl.semaphore_signal(barrier, inc=1, device_id=(b, h - 1, s), device_id_type=MESH)

    @pl.when(h < n_line - 1)
    def _():
        pl.semaphore_signal(barrier, inc=1, device_id=(b, h + 1, s), device_id_type=MESH)

    ends = (h == 0).astype(jnp.int32) + (h == n_line - 1).astype(jnp.int32)
    pl.semaphore_wait(barrier, n_batch + 2 - ends)


def tiles(count, step):
    lax.fori_loop(0, count, lambda i, carry: (step(i), carry)[1], 0)


def rows_at(i, size=TILE):
    return pl.ds(pl.multiple_of(i * size, size), size)


def dot(left, right):
    return jnp.dot(left, right, preferred_element_type=jnp.float32)


def update_statistics(old, left, right, own, sent, worst, s, beside):
    half = old.shape[0] // 2
    worst[...] = jnp.zeros_like(worst)

    def step(i):
        at = rows_at(i)
        new = STAT_DECAY * old[at, :] + (1.0 - STAT_DECAY) / BLOCK * dot(left[at, :], right[...])
        old[at, :] = new
        worst[...] = jnp.maximum(
            worst[...], jnp.max(jnp.sum(jnp.abs(new), axis=1, keepdims=True), axis=0, keepdims=True)
        )
        beside(i)

    tiles(old.shape[0] // TILE, step)

    def split(i):
        here = rows_at(i)
        first = pl.multiple_of(s * half + i * TILE, TILE)
        other = pl.multiple_of((1 - s) * half + i * TILE, TILE)
        own[here, :] = old[pl.ds(first, TILE), :].astype(own.dtype)
        sent[here, :] = old[pl.ds(other, TILE), :].astype(sent.dtype)

    tiles(half // TILE, split)


def series(stat, worst, step_one, step_two, step_three, tail, beside):
    size = stat.shape[0]
    scaled = 2.5 / (worst[...] + EPSILON)

    def first(i):
        at = rows_at(i)
        row = lax.broadcasted_iota(jnp.int32, (TILE, size), 0) + i * TILE
        col = lax.broadcasted_iota(jnp.int32, (TILE, size), 1)
        diagonal = jnp.where(row == col, 0.25, 0.0)
        step_one[at, :] = (diagonal - (0.25 * scaled) * stat[at, :]).astype(jnp.bfloat16)

    tiles(size // TILE, first)

    def second(i):
        at = rows_at(i)
        two = dot(step_one[at, :], step_one[...])
        two_low = two.astype(jnp.bfloat16)
        three = dot(two_low, step_one[...])
        step_two[at, :] = two_low
        step_three[at, :] = three.astype(jnp.bfloat16)
        tail[at, :] = (8.75 * step_one[at, :].astype(jnp.float32) + 4.75 * two + three).astype(jnp.bfloat16)
        beside(i)

    tiles(size // TILE, second)
    return jnp.sqrt(jnp.sqrt(scaled))


def root_rows(at, step_one, step_two, step_three, tail):
    f32 = jnp.float32
    return (
        step_one[at, :].astype(f32)
        + 2.5 * step_two[at, :].astype(f32)
        + 7.5 * step_three[at, :].astype(f32)
        + dot(step_three[at, :], tail[...])
    ).astype(jnp.bfloat16)


class Reduction:
    def __init__(self, n_batch, n_line, partial, out, inbox, from_above, from_below, sems):
        self.n_batch, self.n_line = n_batch, n_line
        self.partial, self.out, self.inbox = partial, out, inbox
        self.from_above, self.from_below = from_above, from_below
        self.local, self.swap_send, self.swap_recv, self.line_send, self.line_recv = sems
        self.b, self.h, self.s = position()
        self.tokens = out.shape[0]
        self.rows = self.tokens // PIECES

    def at(self, q):
        return pl.ds(pl.multiple_of(q * self.rows, self.rows), self.rows)

    def piece(self, bb, q):
        return self.inbox.at[bb, self.at(q)]

    def outgoing(self, bb, q):
        return self.partial.at[pl.ds(pl.multiple_of(bb * self.tokens + q * self.rows, self.rows), self.rows)]

    def own(self, q):
        return pltpu.make_async_copy(self.outgoing(self.b, q), self.piece(self.b, q), self.local.at[q])

    def swap(self, bits, q):
        to = flip(self.b, bits)
        return remote(
            self.outgoing(to, q),
            self.piece(self.b, q),
            self.swap_send.at[bits, q],
            self.swap_recv.at[bits, q],
            (to, self.h, self.s),
        )

    def down_slot(self, bb, q):
        return self.from_above.at[bb, self.at(q)]

    def up_slot(self, bb, q):
        return self.from_below.at[bb, self.at(q)]

    def down(self, bb, q, source):
        return remote(
            source,
            self.down_slot(bb, q),
            self.line_send.at[bb, q],
            self.line_recv.at[0, bb, q],
            (self.b, self.h - 1, self.s),
        )

    def up(self, bb, q, source):
        return remote(
            source,
            self.up_slot(bb, q),
            self.line_send.at[bb, q],
            self.line_recv.at[1, bb, q],
            (self.b, self.h + 1, self.s),
        )

    def start(self):
        half = self.n_batch // 2
        for q in range(PIECES):
            self.own(q).start()
        for bits in [half + low for low in range(half)] + list(range(1, half)):
            for q in range(PIECES):
                self.swap(bits, q).start()

    def down_target(self, step):
        half = self.n_batch // 2
        high, low = self.b // half, self.b % half
        other = step ^ half
        return flip(low, step), step + high * (other - step)

    def up_target(self, step):
        half = self.n_batch // 2
        high, low = self.b // half, self.b % half
        other = step ^ half
        return flip(low + half, step), other + high * (step - other)

    def arrive(self, bits, q):
        @pl.when(bits == 0)
        def _():
            self.own(q).wait()

        @pl.when(bits != 0)
        def _():
            slot = self.piece(self.b, q)
            place = (self.b, self.h, self.s)
            remote(slot, slot, self.swap_send.at[bits, q], self.swap_recv.at[bits, q], place).wait_recv()

    def open(self, step, q):
        target, bits = self.down_target(step)

        @pl.when((target < self.h) & (self.h == self.n_line - 1))
        def _():
            self.arrive(bits, q)
            self.down(target, q, self.piece(target, q)).start()

        over, over_bits = self.up_target(step)

        @pl.when((over > self.h) & (self.h == 0))
        def _():
            self.arrive(over_bits, q)
            self.up(over, q, self.piece(over, q)).start()

    def relay(self, step, q):
        h = self.h
        target, bits = self.down_target(step)
        over, over_bits = self.up_target(step)

        def add(slot, owner):
            slot[...] = (
                slot[...].astype(jnp.float32) + self.piece(owner, q)[...].astype(jnp.float32)
            ).astype(slot.dtype)

        @pl.when(target == h)
        def _():
            self.arrive(bits, q)

        @pl.when((target < h) & (h < self.n_line - 1))
        def _():
            self.arrive(bits, q)
            slot = self.down_slot(target, q)
            move = self.down(target, q, slot)
            move.wait_recv()
            add(slot, target)
            move.start()

        @pl.when((over > h) & (h > 0))
        def _():
            self.arrive(over_bits, q)
            slot = self.up_slot(over, q)
            move = self.up(over, q, slot)
            move.wait_recv()
            add(slot, over)
            move.start()

    def close(self, q):
        h, out, at = self.h, self.out, self.at(q)
        out[at, :] = self.piece(h, q)[...]

        @pl.when(h < self.n_line - 1)
        def _():
            slot = self.down_slot(h, q)
            self.down(h, q, slot).wait_recv()
            out[at, :] = (out[at, :].astype(jnp.float32) + slot[...].astype(jnp.float32)).astype(out.dtype)

        @pl.when(h > 0)
        def _():
            slot = self.up_slot(h, q)
            self.up(h, q, slot).wait_recv()
            out[at, :] = (out[at, :].astype(jnp.float32) + slot[...].astype(jnp.float32)).astype(out.dtype)

    def sent(self, q):
        for bits in range(1, self.n_batch):
            self.swap(bits, q).wait_send()
        for bb in range(self.n_line):
            @pl.when(self.h > bb)
            def _():
                self.down(bb, q, self.down_slot(bb, q)).wait_send()

            @pl.when(self.h < bb)
            def _():
                self.up(bb, q, self.up_slot(bb, q)).wait_send()


def step_kernel(n_batch, n_line, *refs):
    acts_ref, cot_ref, weight_ref, left_ref, right_ref = refs[0:5]
    first_out, second_out = refs[5:7]
    own_out, got_out = refs[7:10], refs[10:13]
    acts_all, weight_all, cot_line, cot_all, grad, turned = refs[13:19]
    left, right, one, two, three, tail, root = refs[19:26]
    partials = refs[26:28]
    inbox, from_above, from_below, own_rows, sent_rows, worst, squares = refs[28:35]
    worst_right = refs[53]
    local_sem, acts_send, acts_recv, weight_send, weight_recv = refs[35:40]
    line_send, line_recv, swap_send, swap_recv, swap_local = refs[40:45]
    side_send, side_recv, own_sem = refs[45:48]
    sums = refs[48:53]
    b, h, s = position()
    tokens, feats = acts_ref.shape
    outs = cot_ref.shape[0]
    rows = outs // PIECES
    reductions = [
        Reduction(
            n_batch,
            n_line,
            partials[p],
            (first_out, second_out)[p],
            inbox.at[p],
            from_above.at[p],
            from_below.at[p],
            [sem.at[p] for sem in sums],
        )
        for p in range(2)
    ]

    def acts_slot(bb, ss):
        return acts_all.at[
            pl.ds(pl.multiple_of(bb * tokens, tokens), tokens),
            pl.ds(pl.multiple_of(ss * feats, feats), feats),
        ]

    def weight_from(ss):
        return weight_ref.at[:, pl.ds(pl.multiple_of(ss * outs, outs), outs)]

    def weight_slot(ss):
        return weight_all.at[pl.ds(pl.multiple_of(ss * feats, feats), feats), :]

    own_cot = pltpu.make_async_copy(cot_ref, cot_line.at[h], local_sem.at[0])
    own_acts = pltpu.make_async_copy(acts_ref, acts_slot(b, s), local_sem.at[1])
    own_weight = pltpu.make_async_copy(weight_from(s), weight_slot(s), local_sem.at[2])
    left_in = pltpu.make_async_copy(left_ref.at[0, s], left, local_sem.at[3])
    right_in = pltpu.make_async_copy(right_ref.at[0, s], right, local_sem.at[4])
    own_cot.start()
    own_acts.start()
    line_barrier(n_batch, n_line)
    own_weight.start()
    right_in.start()
    left_in.start()
    own_acts.wait()
    own_cot.wait()

    def line_slot(hp, q):
        return cot_line.at[hp, pl.ds(q * rows, rows)]

    def up(hp, q):
        return remote(
            line_slot(hp, q), line_slot(hp, q), line_send.at[0, hp, q], line_recv.at[hp, q], (b, h + 1, s)
        )

    def down(hp, q):
        return remote(
            line_slot(hp, q), line_slot(hp, q), line_send.at[1, hp, q], line_recv.at[hp, q], (b, h - 1, s)
        )

    def swap_slot(bb, q):
        return cot_all.at[rows_at(q, rows), pl.ds(pl.multiple_of(bb * tokens, tokens), tokens)]

    def swap(hp, q):
        return remote(
            line_slot(hp, q), swap_slot(b, q), swap_send.at[hp, q], swap_recv.at[b, q], (hp, h, s)
        )

    def swap_here(q):
        return pltpu.make_async_copy(
            cot_line.at[b, rows_at(q, rows)], swap_slot(b, q), swap_local.at[q]
        )

    def pass_on(hp, q):
        @pl.when(hp == b)
        def _():
            swap_here(q).start()

        @pl.when(hp != b)
        def _():
            swap(hp, q).start()

    far = n_batch // 2
    acts_moves = []

    def acts_move(bb, ss, device):
        index = len(acts_moves)
        move = remote(
            acts_slot(bb, ss), acts_slot(bb, ss), acts_send.at[index], acts_recv.at[bb, ss], device
        )
        move.start()
        acts_moves.append(move)

    def acts_wait(bb, ss):
        remote(acts_slot(bb, ss), acts_slot(bb, ss), acts_send.at[0], acts_recv.at[bb, ss], (b, h, s)).wait_recv()

    acts_move(b, s, (flip(b, far), h, s))
    acts_move(b, s, (b, h, 1 - s))
    for q in range(PIECES):
        @pl.when(h < n_line - 1)
        def _():
            up(h, q).start()

        @pl.when(h > 0)
        def _():
            down(h, q).start()

    near = [bits for bits in range(1, far)]
    for bits in near:
        acts_move(b, s, (flip(b, bits), h, s))
    for q in range(PIECES):
        pass_on(h, q)
    acts_wait(flip(b, far), s)
    acts_move(flip(b, far), s, (b, h, 1 - s))
    for bits in near:
        acts_move(flip(b, far), s, (flip(b, bits), h, s))
    weight_move = remote(weight_from(1 - s), weight_slot(s), weight_send, weight_recv, (b, h, 1 - s))
    weight_move.start()
    for place in (b, flip(b, far)):
        acts_wait(place, 1 - s)
        for bits in near:
            acts_move(place, 1 - s, (flip(b, bits), h, s))

    for distance in range(1, n_line):
        for q in range(PIECES):
            @pl.when(h >= distance)
            def _():
                hp = h - distance
                up(hp, q).wait_recv()

                @pl.when(h < n_line - 1)
                def _():
                    up(hp, q).start()

                pass_on(hp, q)

            @pl.when(h + distance < n_line)
            def _():
                hp = h + distance
                down(hp, q).wait_recv()

                @pl.when(h > 0)
                def _():
                    down(hp, q).start()

                pass_on(hp, q)

    for bits in near:
        for place in (flip(b, bits), flip(b, bits + far)):
            for ss in range(2):
                acts_wait(place, ss)
    own_weight.wait()
    weight_move.wait_recv()

    def forward(partial, block_weight):
        def step(i):
            at = rows_at(i)
            partial[at, :] = dot(acts_all[at, :], block_weight[...]).astype(jnp.bfloat16)

        tiles(acts_all.shape[0] // TILE, step)

    forward(partials[0], weight_all)
    first, second = reductions
    first.start()

    def grad_rows(q):
        swap_here(q).wait()
        for bits in range(1, n_batch):
            place = flip(b, bits)
            remote(
                swap_slot(place, q), swap_slot(place, q), swap_send.at[0, q], swap_recv.at[place, q], (b, h, s)
            ).wait_recv()
        at = rows_at(q, rows)
        value = dot(cot_all[at, :], acts_all[...]).astype(jnp.bfloat16)
        grad[at, :] = value
        turned[:, at] = value.T

    tiles(PIECES, grad_rows)

    own_moves, side_moves = [], []

    def exchange(i):
        own = pltpu.make_async_copy(own_rows.at[i], own_out[i], own_sem.at[i])
        side = remote(sent_rows.at[i], got_out[i], side_send.at[i], side_recv.at[i], (b, h, 1 - s))
        own.start()
        side.start()
        own_moves.append(own)
        side_moves.append(side)

    def pieces(i):
        per = PIECES * TILE // BLOCK
        return [i * per + q for q in range(per)]

    def beside_right(i):
        first.open(0, i)

    def beside_left(i):
        first.open(0, PIECES // 2 + i)

    right_in.wait()
    update_statistics(right, grad, turned, own_rows.at[1], sent_rows.at[1], worst_right, s, beside_right)
    exchange(1)
    left_in.wait()
    update_statistics(left, turned, grad, own_rows.at[0], sent_rows.at[0], worst, s, beside_left)
    exchange(0)

    def right_powers(i):
        first.open(1, i)
        for q in pieces(i):
            first.relay(0, q)

    scale_right = series(right, worst_right, one, two, three, tail, right_powers)

    def right_root(i):
        root[rows_at(i), :] = root_rows(rows_at(i), one, two, three, tail)
        first.open(1, PIECES // 2 + i)

    tiles(BLOCK // TILE, right_root)

    def left_powers(i):
        for q in pieces(i):
            first.open(2, q)
            first.relay(1, q)

    scale = series(left, worst, one, two, three, tail, left_powers) * scale_right
    squares[...] = jnp.zeros_like(squares)
    update = left

    def apply(i):
        at = rows_at(i)
        left_rows = root_rows(at, one, two, three, tail)
        mixed = turned[at, :].astype(jnp.float32) + dot(left_rows, turned[...])
        value = mixed + dot(mixed.astype(jnp.bfloat16), root[...])
        update[at, :] = value
        squares[...] += jnp.sum(jnp.sum(value * value, axis=1, keepdims=True), axis=0, keepdims=True)
        for q in pieces(i):
            first.open(3, q)
            first.relay(2, q)

    tiles(BLOCK // TILE, apply)
    scaled = scale / jnp.sqrt(scale * scale * squares[...] / (BLOCK * BLOCK) + EPSILON)
    half = BLOCK // 2

    def finish(i):
        at = rows_at(i)
        root[at, :] = (
            weight_all[at, :].astype(jnp.float32) - LEARN_RATE * (scaled * update[at, :])
        ).astype(jnp.bfloat16)

    tiles(BLOCK // TILE, finish)
    forward(partials[1], root)
    second.start()

    def split(i):
        here = rows_at(i)
        mine = pl.multiple_of(s * half + i * TILE, TILE)
        other = pl.multiple_of((1 - s) * half + i * TILE, TILE)
        own_rows[2, here, :] = (scaled * update[pl.ds(mine, TILE), :]).astype(jnp.bfloat16)
        sent_rows[2, here, :] = (scaled * update[pl.ds(other, TILE), :]).astype(jnp.bfloat16)

    tiles(half // TILE, split)
    exchange(2)

    tiles(PIECES, lambda q: first.relay(3, q))
    for step in range(n_batch):
        def both(q):
            second.open(step, q)
            second.relay(step, q)

        tiles(PIECES, both)
    tiles(PIECES, first.close)
    tiles(PIECES, second.close)

    for move in acts_moves:
        move.wait_send()
    weight_move.wait_send()
    for hp in range(n_line):
        for q in range(PIECES):
            @pl.when((hp <= h) & (h < n_line - 1))
            def _():
                up(hp, q).wait_send()

            @pl.when((hp >= h) & (h > 0))
            def _():
                down(hp, q).wait_send()

            @pl.when(hp != b)
            def _():
                swap(hp, q).wait_send()
    for reduction in reductions:
        tiles(PIECES, reduction.sent)
    for move in own_moves:
        move.wait()
    for move in side_moves:
        move.wait()


def block_step(activations, cotangent, weight, left_old, right_old, n_batch, n_line):
    tokens, feats = activations.shape
    outs = cotangent.shape[0]
    all_tokens, half = n_batch * tokens, BLOCK // 2
    vmem = pl.BlockSpec(memory_space=pltpu.VMEM)
    hbm = pl.BlockSpec(memory_space=pl.ANY)
    sem = pltpu.SemaphoreType.DMA
    bf, f32 = jnp.bfloat16, jnp.float32
    out = jax.ShapeDtypeStruct((tokens, outs), bf)
    part = jax.ShapeDtypeStruct((half, BLOCK), bf)
    low, wide = pltpu.VMEM((BLOCK, BLOCK), bf), pltpu.VMEM((BLOCK, BLOCK), f32)
    partial = pltpu.VMEM((all_tokens, outs), bf)
    return pl.pallas_call(
        functools.partial(step_kernel, n_batch, n_line),
        out_shape=(out, out) + (part,) * 6,
        in_specs=[hbm] * 5,
        out_specs=(vmem,) * 2 + (hbm,) * 6,
        scratch_shapes=[
            pltpu.VMEM((all_tokens, BLOCK), bf),
            low,
            pltpu.VMEM((n_line, outs, tokens), bf),
            pltpu.VMEM((outs, all_tokens), bf),
            low,
            low,
            wide,
            wide,
            low,
            low,
            low,
            low,
            low,
            partial,
            partial,
            pltpu.VMEM((2, n_batch, tokens, outs), bf),
            pltpu.VMEM((2, n_line, tokens, outs), bf),
            pltpu.VMEM((2, n_line, tokens, outs), bf),
            pltpu.VMEM((3, half, BLOCK), bf),
            pltpu.VMEM((3, half, BLOCK), bf),
            pltpu.VMEM((1, 1), f32),
            pltpu.VMEM((1, 1), f32),
            sem((5,)),
            sem((2 * n_batch - 1,)),
            sem((n_batch, 2)),
            sem,
            sem,
            sem((2, n_line, PIECES)),
            sem((n_line, PIECES)),
            sem((n_line, PIECES)),
            sem((n_batch, PIECES)),
            sem((PIECES,)),
            sem((3,)),
            sem((3,)),
            sem((3,)),
            sem((2, PIECES)),
            sem((2, n_batch, PIECES)),
            sem((2, n_batch, PIECES)),
            sem((2, n_line, PIECES)),
            sem((2, 2, n_line, PIECES)),
            pltpu.VMEM((1, 1), f32),
        ],
        compiler_params=pltpu.CompilerParams(
            collective_id=0, has_side_effects=True, vmem_limit_bytes=VMEM_LIMIT
        ),
        name="block_step",
    )(activations, cotangent, weight, left_old, right_old)


ASSEMBLE_STEPS = 2


def assemble_kernel(
    left_own, right_own, direction_own, left_got, right_got, direction_got, first_in, second_in,
    first, left, right, direction, second,
):
    s = lax.axis_index("solver")
    width = direction_own.shape[1]
    for own, got, out in ((left_own, left_got, left), (right_own, right_got, right)):
        out[0, s] = own[...].astype(jnp.float32)
        out[0, 1 - s] = got[...].astype(jnp.float32)
    direction[:, pl.ds(pl.multiple_of(s * width, width), width)] = direction_own[...].astype(jnp.float32)
    direction[:, pl.ds(pl.multiple_of((1 - s) * width, width), width)] = direction_got[...].astype(jnp.float32)
    first[...] = first_in[...].T
    second[...] = second_in[...].T


def assemble(rows, first, second):
    half, width = rows[0].shape
    tokens, outs = first.shape
    step = half // ASSEMBLE_STEPS
    cols = outs // ASSEMBLE_STEPS
    f32 = jnp.float32
    part = pl.BlockSpec((step, width), lambda i: (i, 0))
    stat = pl.BlockSpec((1, 2, step, width), lambda i: (0, 0, i, 0))
    turned_in = pl.BlockSpec((tokens, cols), lambda i: (0, i))
    turned_out = pl.BlockSpec((cols, tokens), lambda i: (i, 0))
    return pl.pallas_call(
        assemble_kernel,
        grid=(ASSEMBLE_STEPS,),
        out_shape=(
            jax.ShapeDtypeStruct((outs, tokens), first.dtype),
            jax.ShapeDtypeStruct((1, 2, half, width), f32),
            jax.ShapeDtypeStruct((1, 2, half, width), f32),
            jax.ShapeDtypeStruct((half, 2 * width), f32),
            jax.ShapeDtypeStruct((outs, tokens), first.dtype),
        ),
        in_specs=[part] * 6 + [turned_in] * 2,
        out_specs=(turned_out, stat, stat, pl.BlockSpec((step, 2 * width), lambda i: (i, 0)), turned_out),
        compiler_params=pltpu.CompilerParams(vmem_limit_bytes=VMEM_LIMIT),
        name="assemble",
    )(*rows, first, second)


def owned_body(activations, cotangent, weight, left_old, right_old, *, n_batch, n_line):
    first, second, *rows = block_step(
        activations, cotangent, weight, left_old, right_old, n_batch, n_line
    )
    return assemble(rows, first, second)


def solution(mesh):
    in_specs = (
        P("batch", ("hidden", "solver")),
        P(("hidden", "solver"), "batch"),
        P(("hidden", "solver"), "batch"),
        P("hidden", "batch", None, None),
        P("hidden", "batch", None, None),
    )
    out_specs = (
        P(("hidden", "solver"), "batch"),
        P("hidden", "batch", "solver", None),
        P("hidden", "batch", "solver", None),
        P(("hidden", "solver"), "batch"),
        P(("hidden", "solver"), "batch"),
    )
    n_batch = mesh.shape["batch"]
    n_feat = mesh.shape["hidden"] * mesh.shape["solver"]

    n_line = mesh.shape["hidden"]
    n_solver = mesh.shape["solver"]

    def owned(activations, cotangent, weight, left_old, right_old):
        blocks = left_old.shape[1]
        even = n_line == n_batch == 2 * n_solver
        return even and n_solver == 2 and blocks == n_solver and cotangent.shape[0] == BLOCK

    def step(activations, cotangent, weight, left_old, right_old):
        args = (activations, cotangent, weight, left_old, right_old)
        if owned(*args):
            return owned_body(*args, n_batch=n_batch, n_line=n_line)
        return body(
            activations,
            cotangent,
            weight,
            left_old,
            right_old,
            n_batch=n_batch,
            n_solver=mesh.shape["solver"],
            n_feat=n_feat,
        )

    return jax.shard_map(step, mesh=mesh, in_specs=in_specs, out_specs=out_specs, check_vma=False)
```

```python
import functools

import jax
import jax.numpy as jnp
from jax import lax
from jax.experimental import pallas as pl
from jax.experimental.pallas import tpu as pltpu
from jax.sharding import PartitionSpec as P

BLOCK = 1024


STAT_DECAY = 0.8
LEARN_RATE = 0.005
EPSILON = 1e-06

ALL = ("batch", "hidden", "solver")
FEATURES = ("hidden", "solver")


def product(left_mat, right_mat):
    return jnp.einsum("bij,bjk->bik", left_mat, right_mat, preferred_element_type=jnp.float32)


def prepare(factor):
    identity = jnp.eye(BLOCK, dtype=jnp.float32)
    scaled = 2.5 / (jnp.max(jnp.sum(jnp.abs(factor), axis=2), axis=1) + EPSILON)
    moment = scaled[:, None, None] * factor
    newton_step = (5.0 * identity - moment) * 0.25
    return (scaled, moment.astype(jnp.bfloat16), newton_step.astype(jnp.bfloat16))


def apply_root(start, moment, step):
    power = start
    for _ in range(4):
        power = product(power.astype(jnp.bfloat16), step)
    power = product(power.astype(jnp.bfloat16), moment)
    return (5.0 * start.astype(jnp.float32) - power) * 0.25


def body(activations, cotangent, weight, left_old, right_old, *, n_batch, n_solver, n_feat):
    rows_here = weight.shape[0]
    nblocks = weight.shape[1] // BLOCK
    per_batch = n_feat // n_batch
    out_rows = weight.shape[1] // per_batch
    tokens = activations.shape[0]
    to_owner = [
        (b * n_feat + c * n_batch + t, t * n_feat + b * per_batch + c)
        for b in range(n_batch)
        for c in range(per_batch)
        for t in range(n_batch)
    ]
    from_owner = [(target, source) for source, target in to_owner]

    def partial_forward(weight_here):
        split = weight_here.reshape(rows_here, per_batch, out_rows)
        out = jnp.einsum("fco,btf->cbot", split, acts_all, preferred_element_type=jnp.float32)
        return out.astype(jnp.bfloat16).reshape(n_feat * out_rows, tokens)

    def reduce_forward(partial):
        return lax.psum_scatter(partial, FEATURES, scatter_dimension=0, tiled=True)

    acts_all = lax.all_gather(activations, "batch", axis=0, tiled=False)
    here = lax.axis_index("solver")
    acts_block = jnp.zeros((n_batch, tokens, n_solver * rows_here), acts_all.dtype)
    for shift in range(n_solver):
        part = acts_all
        if shift > 0:
            pairs = [(at, (at + shift) % n_solver) for at in range(n_solver)]
            part = lax.ppermute(acts_all, "solver", pairs)
        first_col = lax.rem(here + n_solver - shift, n_solver) * rows_here
        acts_block = lax.dynamic_update_slice_in_dim(acts_block, part, first_col, 2)
    cot_moved = lax.ppermute(cotangent, ALL, from_owner)
    cot_all = lax.all_gather(cot_moved, FEATURES, axis=0, tiled=False)
    cot_all = cot_all.reshape(per_batch, n_batch, out_rows, tokens)
    first_partial = partial_forward(weight)
    first_partial, cot_all = lax.optimization_barrier((first_partial, cot_all))
    first_sum = reduce_forward(first_partial)
    grad_full = jnp.einsum("cbot,btf->cof", cot_all, acts_block, preferred_element_type=jnp.float32)
    grad_full = grad_full.astype(jnp.bfloat16).reshape(nblocks, BLOCK, BLOCK)
    gram_left = jnp.einsum("bnm,bnk->bmk", grad_full, grad_full, preferred_element_type=jnp.float32)
    gram_right = jnp.einsum(
        "bnm,bkm->bnk", grad_full, grad_full, preferred_element_type=jnp.float32
    )
    left_all = STAT_DECAY * left_old[0] + (1.0 - STAT_DECAY) / BLOCK * gram_left
    right_all = STAT_DECAY * right_old[0] + (1.0 - STAT_DECAY) / BLOCK * gram_right
    first_row = lax.axis_index("solver") * rows_here
    new_left = lax.dynamic_slice_in_dim(left_all, first_row, rows_here, 1)[None]
    new_right = lax.dynamic_slice_in_dim(right_all, first_row, rows_here, 1)[None]
    scale_left, moment_left, step_left = prepare(left_all)
    own_rows = lax.dynamic_slice_in_dim(step_left, first_row, rows_here, 1)
    root_rows = apply_root(own_rows, moment_left, step_left)
    mixed_rows = jnp.einsum(
        "brm,bnm->brn",
        root_rows.astype(jnp.bfloat16),
        grad_full,
        preferred_element_type=jnp.float32,
    )
    scale_right, moment_right, step_right = prepare(right_all)
    turned = product(mixed_rows.astype(jnp.bfloat16), step_right)
    scale_both = (scale_left**0.25) * (scale_right**0.25)
    update = scale_both[:, None, None] * apply_root(turned, moment_right, step_right)
    update, first_sum = lax.optimization_barrier((update, first_sum))
    first_out = lax.ppermute(first_sum, ALL, to_owner)
    squares = lax.psum(jnp.sum(update * update, axis=(1, 2)), "solver")
    spread = jnp.sqrt(squares / (BLOCK * BLOCK) + EPSILON)
    scaled_update = update / spread[:, None, None]
    direction = jnp.transpose(scaled_update, (1, 0, 2)).reshape(rows_here, nblocks * BLOCK)
    new_weight = (weight.astype(jnp.float32) - LEARN_RATE * direction).astype(jnp.bfloat16)
    second_sum = reduce_forward(partial_forward(new_weight))
    second_sum, new_left, new_right = lax.optimization_barrier((second_sum, new_left, new_right))
    second_out = lax.ppermute(second_sum, ALL, to_owner)
    return (first_out, new_left, new_right, direction, second_out)


MESH = pl.DeviceIdType.MESH
VMEM_LIMIT = 62 * 1024 * 1024
PIECES = 4
TILE = 512


def remote(src, dst, send_sem, recv_sem, device):
    return pltpu.make_async_remote_copy(
        src_ref=src,
        dst_ref=dst,
        send_sem=send_sem,
        recv_sem=recv_sem,
        device_id=device,
        device_id_type=MESH,
    )


def position():
    return lax.axis_index("batch"), lax.axis_index("hidden"), lax.axis_index("solver")


def flip(index, bits):
    bit = 1
    while bit <= bits:
        if bits & bit:
            index = index + bit * (1 - 2 * ((index // bit) % 2))
        bit *= 2
    return index


def line_barrier(n_batch, n_line):
    b, h, s = position()
    barrier = pltpu.get_barrier_semaphore()
    for bits in range(1, n_batch):
        pl.semaphore_signal(barrier, inc=1, device_id=(flip(b, bits), h, s), device_id_type=MESH)
    pl.semaphore_signal(barrier, inc=1, device_id=(b, h, 1 - s), device_id_type=MESH)

    @pl.when(h > 0)
    def _():
        pl.semaphore_signal(barrier, inc=1, device_id=(b, h - 1, s), device_id_type=MESH)

    @pl.when(h < n_line - 1)
    def _():
        pl.semaphore_signal(barrier, inc=1, device_id=(b, h + 1, s), device_id_type=MESH)

    ends = (h == 0).astype(jnp.int32) + (h == n_line - 1).astype(jnp.int32)
    pl.semaphore_wait(barrier, n_batch + 2 - ends)


def tiles(count, step):
    lax.fori_loop(0, count, lambda i, carry: (step(i), carry)[1], 0)


def rows_at(i, size=TILE):
    return pl.ds(pl.multiple_of(i * size, size), size)


def dot(left, right):
    return jnp.dot(left, right, preferred_element_type=jnp.float32)


def update_statistics(old, left, right, own, sent, worst, s, beside):
    half = old.shape[0] // 2
    worst[...] = jnp.zeros_like(worst)

    def step(i):
        at = rows_at(i)
        new = STAT_DECAY * old[at, :] + (1.0 - STAT_DECAY) / BLOCK * dot(left[at, :], right[...])
        old[at, :] = new
        worst[...] = jnp.maximum(
            worst[...], jnp.max(jnp.sum(jnp.abs(new), axis=1, keepdims=True), axis=0, keepdims=True)
        )
        beside(i)

    tiles(old.shape[0] // TILE, step)

    def split(i):
        here = rows_at(i)
        first = pl.multiple_of(s * half + i * TILE, TILE)
        other = pl.multiple_of((1 - s) * half + i * TILE, TILE)
        own[here, :] = old[pl.ds(first, TILE), :].astype(own.dtype)
        sent[here, :] = old[pl.ds(other, TILE), :].astype(sent.dtype)

    tiles(half // TILE, split)


def series(stat, worst, step_one, step_two, step_three, tail, beside):
    size = stat.shape[0]
    scaled = 2.5 / (worst[...] + EPSILON)

    def first(i):
        at = rows_at(i)
        row = lax.broadcasted_iota(jnp.int32, (TILE, size), 0) + i * TILE
        col = lax.broadcasted_iota(jnp.int32, (TILE, size), 1)
        diagonal = jnp.where(row == col, 0.25, 0.0)
        step_one[at, :] = (diagonal - (0.25 * scaled) * stat[at, :]).astype(jnp.bfloat16)

    tiles(size // TILE, first)

    def second(i):
        at = rows_at(i)
        two = dot(step_one[at, :], step_one[...])
        two_low = two.astype(jnp.bfloat16)
        three = dot(two_low, step_one[...])
        step_two[at, :] = two_low
        step_three[at, :] = three.astype(jnp.bfloat16)
        tail[at, :] = (8.75 * step_one[at, :].astype(jnp.float32) + 4.75 * two + three).astype(jnp.bfloat16)
        beside(i)

    tiles(size // TILE, second)
    return jnp.sqrt(jnp.sqrt(scaled))


def root_rows(at, step_one, step_two, step_three, tail):
    f32 = jnp.float32
    return (
        step_one[at, :].astype(f32)
        + 2.5 * step_two[at, :].astype(f32)
        + 7.5 * step_three[at, :].astype(f32)
        + dot(step_three[at, :], tail[...])
    ).astype(jnp.bfloat16)


class Reduction:
    def __init__(self, n_batch, n_line, partial, out, inbox, from_above, from_below, sems):
        self.n_batch, self.n_line = n_batch, n_line
        self.partial, self.out, self.inbox = partial, out, inbox
        self.from_above, self.from_below = from_above, from_below
        self.local, self.swap_send, self.swap_recv, self.line_send, self.line_recv = sems
        self.b, self.h, self.s = position()
        self.tokens = out.shape[0]
        self.rows = self.tokens // PIECES

    def at(self, q):
        return pl.ds(pl.multiple_of(q * self.rows, self.rows), self.rows)

    def piece(self, bb, q):
        return self.inbox.at[bb, self.at(q)]

    def outgoing(self, bb, q):
        return self.partial.at[pl.ds(pl.multiple_of(bb * self.tokens + q * self.rows, self.rows), self.rows)]

    def own(self, q):
        return pltpu.make_async_copy(self.outgoing(self.b, q), self.piece(self.b, q), self.local.at[q])

    def swap(self, bits, q):
        to = flip(self.b, bits)
        return remote(
            self.outgoing(to, q),
            self.piece(self.b, q),
            self.swap_send.at[bits, q],
            self.swap_recv.at[bits, q],
            (to, self.h, self.s),
        )

    def down_slot(self, bb, q):
        return self.from_above.at[bb, self.at(q)]

    def up_slot(self, bb, q):
        return self.from_below.at[bb, self.at(q)]

    def down(self, bb, q, source):
        return remote(
            source,
            self.down_slot(bb, q),
            self.line_send.at[bb, q],
            self.line_recv.at[0, bb, q],
            (self.b, self.h - 1, self.s),
        )

    def up(self, bb, q, source):
        return remote(
            source,
            self.up_slot(bb, q),
            self.line_send.at[bb, q],
            self.line_recv.at[1, bb, q],
            (self.b, self.h + 1, self.s),
        )

    def start(self):
        half = self.n_batch // 2
        for q in range(PIECES):
            self.own(q).start()
        for bits in [half + low for low in range(half)] + list(range(1, half)):
            for q in range(PIECES):
                self.swap(bits, q).start()

    def down_target(self, step):
        half = self.n_batch // 2
        high, low = self.b // half, self.b % half
        other = step ^ half
        return flip(low, step), step + high * (other - step)

    def up_target(self, step):
        half = self.n_batch // 2
        high, low = self.b // half, self.b % half
        other = step ^ half
        return flip(low + half, step), other + high * (step - other)

    def arrive(self, bits, q):
        @pl.when(bits == 0)
        def _():
            self.own(q).wait()

        @pl.when(bits != 0)
        def _():
            slot = self.piece(self.b, q)
            place = (self.b, self.h, self.s)
            remote(slot, slot, self.swap_send.at[bits, q], self.swap_recv.at[bits, q], place).wait_recv()

    def open(self, step, q):
        target, bits = self.down_target(step)

        @pl.when((target < self.h) & (self.h == self.n_line - 1))
        def _():
            self.arrive(bits, q)
            self.down(target, q, self.piece(target, q)).start()

        over, over_bits = self.up_target(step)

        @pl.when((over > self.h) & (self.h == 0))
        def _():
            self.arrive(over_bits, q)
            self.up(over, q, self.piece(over, q)).start()

    def relay(self, step, q):
        h = self.h
        target, bits = self.down_target(step)
        over, over_bits = self.up_target(step)

        def add(slot, owner):
            slot[...] = (
                slot[...].astype(jnp.float32) + self.piece(owner, q)[...].astype(jnp.float32)
            ).astype(slot.dtype)

        @pl.when(target == h)
        def _():
            self.arrive(bits, q)

        @pl.when((target < h) & (h < self.n_line - 1))
        def _():
            self.arrive(bits, q)
            slot = self.down_slot(target, q)
            move = self.down(target, q, slot)
            move.wait_recv()
            add(slot, target)
            move.start()

        @pl.when((over > h) & (h > 0))
        def _():
            self.arrive(over_bits, q)
            slot = self.up_slot(over, q)
            move = self.up(over, q, slot)
            move.wait_recv()
            add(slot, over)
            move.start()

    def close(self, q):
        h, out, at = self.h, self.out, self.at(q)
        out[at, :] = self.piece(h, q)[...]

        @pl.when(h < self.n_line - 1)
        def _():
            slot = self.down_slot(h, q)
            self.down(h, q, slot).wait_recv()
            out[at, :] = (out[at, :].astype(jnp.float32) + slot[...].astype(jnp.float32)).astype(out.dtype)

        @pl.when(h > 0)
        def _():
            slot = self.up_slot(h, q)
            self.up(h, q, slot).wait_recv()
            out[at, :] = (out[at, :].astype(jnp.float32) + slot[...].astype(jnp.float32)).astype(out.dtype)

    def sent(self, q):
        for bits in range(1, self.n_batch):
            self.swap(bits, q).wait_send()
        for bb in range(self.n_line):
            @pl.when(self.h > bb)
            def _():
                self.down(bb, q, self.down_slot(bb, q)).wait_send()

            @pl.when(self.h < bb)
            def _():
                self.up(bb, q, self.up_slot(bb, q)).wait_send()


def step_kernel(n_batch, n_line, *refs):
    acts_ref, cot_ref, weight_ref, left_ref, right_ref = refs[0:5]
    first_out, second_out = refs[5:7]
    own_out, got_out = refs[7:10], refs[10:13]
    acts_all, weight_all, cot_line, cot_all, grad, turned = refs[13:19]
    left, right, one, two, three, tail, root = refs[19:26]
    partials = refs[26:28]
    inbox, from_above, from_below, own_rows, sent_rows, worst, squares = refs[28:35]
    worst_right = refs[53]
    local_sem, acts_send, acts_recv, weight_send, weight_recv = refs[35:40]
    line_send, line_recv, swap_send, swap_recv, swap_local = refs[40:45]
    side_send, side_recv, own_sem = refs[45:48]
    sums = refs[48:53]
    b, h, s = position()
    tokens, feats = acts_ref.shape
    outs = cot_ref.shape[0]
    rows = outs // PIECES
    reductions = [
        Reduction(
            n_batch,
            n_line,
            partials[p],
            (first_out, second_out)[p],
            inbox.at[p],
            from_above.at[p],
            from_below.at[p],
            [sem.at[p] for sem in sums],
        )
        for p in range(2)
    ]

    def acts_slot(bb, ss):
        return acts_all.at[
            pl.ds(pl.multiple_of(bb * tokens, tokens), tokens),
            pl.ds(pl.multiple_of(ss * feats, feats), feats),
        ]

    def weight_from(ss):
        return weight_ref.at[:, pl.ds(pl.multiple_of(ss * outs, outs), outs)]

    def weight_slot(ss):
        return weight_all.at[pl.ds(pl.multiple_of(ss * feats, feats), feats), :]

    own_cot = pltpu.make_async_copy(cot_ref, cot_line.at[h], local_sem.at[0])
    own_acts = pltpu.make_async_copy(acts_ref, acts_slot(b, s), local_sem.at[1])
    own_weight = pltpu.make_async_copy(weight_from(s), weight_slot(s), local_sem.at[2])
    left_in = pltpu.make_async_copy(left_ref.at[0, s], left, local_sem.at[3])
    right_in = pltpu.make_async_copy(right_ref.at[0, s], right, local_sem.at[4])
    own_cot.start()
    own_acts.start()
    line_barrier(n_batch, n_line)
    own_weight.start()
    right_in.start()
    left_in.start()
    own_acts.wait()
    own_cot.wait()

    def line_slot(hp, q):
        return cot_line.at[hp, pl.ds(q * rows, rows)]

    def up(hp, q):
        return remote(
            line_slot(hp, q), line_slot(hp, q), line_send.at[0, hp, q], line_recv.at[hp, q], (b, h + 1, s)
        )

    def down(hp, q):
        return remote(
            line_slot(hp, q), line_slot(hp, q), line_send.at[1, hp, q], line_recv.at[hp, q], (b, h - 1, s)
        )

    def swap_slot(bb, q):
        return cot_all.at[rows_at(q, rows), pl.ds(pl.multiple_of(bb * tokens, tokens), tokens)]

    def swap(hp, q):
        return remote(
            line_slot(hp, q), swap_slot(b, q), swap_send.at[hp, q], swap_recv.at[b, q], (hp, h, s)
        )

    def swap_here(q):
        return pltpu.make_async_copy(
            cot_line.at[b, rows_at(q, rows)], swap_slot(b, q), swap_local.at[q]
        )

    def pass_on(hp, q):
        @pl.when(hp == b)
        def _():
            swap_here(q).start()

        @pl.when(hp != b)
        def _():
            swap(hp, q).start()

    far = n_batch // 2
    acts_moves = []

    def acts_move(bb, ss, device):
        index = len(acts_moves)
        move = remote(
            acts_slot(bb, ss), acts_slot(bb, ss), acts_send.at[index], acts_recv.at[bb, ss], device
        )
        move.start()
        acts_moves.append(move)

    def acts_wait(bb, ss):
        remote(acts_slot(bb, ss), acts_slot(bb, ss), acts_send.at[0], acts_recv.at[bb, ss], (b, h, s)).wait_recv()

    acts_move(b, s, (flip(b, far), h, s))
    acts_move(b, s, (b, h, 1 - s))
    for q in range(PIECES):
        @pl.when(h < n_line - 1)
        def _():
            up(h, q).start()

        @pl.when(h > 0)
        def _():
            down(h, q).start()

    near = [bits for bits in range(1, far)]
    for bits in near:
        acts_move(b, s, (flip(b, bits), h, s))
    for q in range(PIECES):
        pass_on(h, q)
    acts_wait(flip(b, far), s)
    acts_move(flip(b, far), s, (b, h, 1 - s))
    for bits in near:
        acts_move(flip(b, far), s, (flip(b, bits), h, s))
    weight_move = remote(weight_from(1 - s), weight_slot(s), weight_send, weight_recv, (b, h, 1 - s))
    weight_move.start()
    for place in (b, flip(b, far)):
        acts_wait(place, 1 - s)
        for bits in near:
            acts_move(place, 1 - s, (flip(b, bits), h, s))

    for distance in range(1, n_line):
        for q in range(PIECES):
            @pl.when(h >= distance)
            def _():
                hp = h - distance
                up(hp, q).wait_recv()

                @pl.when(h < n_line - 1)
                def _():
                    up(hp, q).start()

                pass_on(hp, q)

            @pl.when(h + distance < n_line)
            def _():
                hp = h + distance
                down(hp, q).wait_recv()

                @pl.when(h > 0)
                def _():
                    down(hp, q).start()

                pass_on(hp, q)

    for bits in near:
        for place in (flip(b, bits), flip(b, bits + far)):
            for ss in range(2):
                acts_wait(place, ss)
    own_weight.wait()
    weight_move.wait_recv()

    def forward(partial, block_weight):
        def step(i):
            at = rows_at(i)
            partial[at, :] = dot(acts_all[at, :], block_weight[...]).astype(jnp.bfloat16)

        tiles(acts_all.shape[0] // TILE, step)

    forward(partials[0], weight_all)
    first, second = reductions
    first.start()

    def grad_rows(q):
        swap_here(q).wait()
        for bits in range(1, n_batch):
            place = flip(b, bits)
            remote(
                swap_slot(place, q), swap_slot(place, q), swap_send.at[0, q], swap_recv.at[place, q], (b, h, s)
            ).wait_recv()
        at = rows_at(q, rows)
        value = dot(cot_all[at, :], acts_all[...]).astype(jnp.bfloat16)
        grad[at, :] = value
        turned[:, at] = value.T

    tiles(PIECES, grad_rows)

    own_moves, side_moves = [], []

    def exchange(i):
        own = pltpu.make_async_copy(own_rows.at[i], own_out[i], own_sem.at[i])
        side = remote(sent_rows.at[i], got_out[i], side_send.at[i], side_recv.at[i], (b, h, 1 - s))
        own.start()
        side.start()
        own_moves.append(own)
        side_moves.append(side)

    def pieces(i):
        per = PIECES * TILE // BLOCK
        return [i * per + q for q in range(per)]

    def beside_right(i):
        first.open(0, i)

    def beside_left(i):
        first.open(0, PIECES // 2 + i)

    right_in.wait()
    update_statistics(right, grad, turned, own_rows.at[1], sent_rows.at[1], worst_right, s, beside_right)
    exchange(1)
    left_in.wait()
    update_statistics(left, turned, grad, own_rows.at[0], sent_rows.at[0], worst, s, beside_left)
    exchange(0)

    def right_powers(i):
        first.open(1, i)

    scale_right = series(right, worst_right, one, two, three, tail, right_powers)

    def right_root(i):
        root[rows_at(i), :] = root_rows(rows_at(i), one, two, three, tail)
        for q in pieces(i):
            first.relay(0, q)
        first.open(1, PIECES // 2 + i)

    tiles(BLOCK // TILE, right_root)

    def left_powers(i):
        for q in pieces(i):
            first.open(2, q)
            first.relay(1, q)

    scale = series(left, worst, one, two, three, tail, left_powers) * scale_right
    squares[...] = jnp.zeros_like(squares)
    update = left

    def apply(i):
        at = rows_at(i)
        left_rows = root_rows(at, one, two, three, tail)
        mixed = turned[at, :].astype(jnp.float32) + dot(left_rows, turned[...])
        value = mixed + dot(mixed.astype(jnp.bfloat16), root[...])
        update[at, :] = value
        squares[...] += jnp.sum(jnp.sum(value * value, axis=1, keepdims=True), axis=0, keepdims=True)
        for q in pieces(i):
            first.open(3, q)
            first.relay(2, q)

    tiles(BLOCK // TILE, apply)
    scaled = scale / jnp.sqrt(scale * scale * squares[...] / (BLOCK * BLOCK) + EPSILON)
    half = BLOCK // 2

    def finish(i):
        at = rows_at(i)
        root[at, :] = (
            weight_all[at, :].astype(jnp.float32) - LEARN_RATE * (scaled * update[at, :])
        ).astype(jnp.bfloat16)

    tiles(BLOCK // TILE, finish)
    forward(partials[1], root)
    second.start()

    def split(i):
        here = rows_at(i)
        mine = pl.multiple_of(s * half + i * TILE, TILE)
        other = pl.multiple_of((1 - s) * half + i * TILE, TILE)
        own_rows[2, here, :] = (scaled * update[pl.ds(mine, TILE), :]).astype(jnp.bfloat16)
        sent_rows[2, here, :] = (scaled * update[pl.ds(other, TILE), :]).astype(jnp.bfloat16)

    tiles(half // TILE, split)
    exchange(2)

    tiles(PIECES, lambda q: first.relay(3, q))
    for step in range(n_batch):
        def both(q):
            second.open(step, q)
            second.relay(step, q)

        tiles(PIECES, both)
    tiles(PIECES, first.close)
    tiles(PIECES, second.close)

    for move in acts_moves:
        move.wait_send()
    weight_move.wait_send()
    for hp in range(n_line):
        for q in range(PIECES):
            @pl.when((hp <= h) & (h < n_line - 1))
            def _():
                up(hp, q).wait_send()

            @pl.when((hp >= h) & (h > 0))
            def _():
                down(hp, q).wait_send()

            @pl.when(hp != b)
            def _():
                swap(hp, q).wait_send()
    for reduction in reductions:
        tiles(PIECES, reduction.sent)
    for move in own_moves:
        move.wait()
    for move in side_moves:
        move.wait()


def block_step(activations, cotangent, weight, left_old, right_old, n_batch, n_line):
    tokens, feats = activations.shape
    outs = cotangent.shape[0]
    all_tokens, half = n_batch * tokens, BLOCK // 2
    vmem = pl.BlockSpec(memory_space=pltpu.VMEM)
    hbm = pl.BlockSpec(memory_space=pl.ANY)
    sem = pltpu.SemaphoreType.DMA
    bf, f32 = jnp.bfloat16, jnp.float32
    out = jax.ShapeDtypeStruct((tokens, outs), bf)
    part = jax.ShapeDtypeStruct((half, BLOCK), bf)
    low, wide = pltpu.VMEM((BLOCK, BLOCK), bf), pltpu.VMEM((BLOCK, BLOCK), f32)
    partial = pltpu.VMEM((all_tokens, outs), bf)
    return pl.pallas_call(
        functools.partial(step_kernel, n_batch, n_line),
        out_shape=(out, out) + (part,) * 6,
        in_specs=[hbm] * 5,
        out_specs=(vmem,) * 2 + (hbm,) * 6,
        scratch_shapes=[
            pltpu.VMEM((all_tokens, BLOCK), bf),
            low,
            pltpu.VMEM((n_line, outs, tokens), bf),
            pltpu.VMEM((outs, all_tokens), bf),
            low,
            low,
            wide,
            wide,
            low,
            low,
            low,
            low,
            low,
            partial,
            partial,
            pltpu.VMEM((2, n_batch, tokens, outs), bf),
            pltpu.VMEM((2, n_line, tokens, outs), bf),
            pltpu.VMEM((2, n_line, tokens, outs), bf),
            pltpu.VMEM((3, half, BLOCK), bf),
            pltpu.VMEM((3, half, BLOCK), bf),
            pltpu.VMEM((1, 1), f32),
            pltpu.VMEM((1, 1), f32),
            sem((5,)),
            sem((2 * n_batch - 1,)),
            sem((n_batch, 2)),
            sem,
            sem,
            sem((2, n_line, PIECES)),
            sem((n_line, PIECES)),
            sem((n_line, PIECES)),
            sem((n_batch, PIECES)),
            sem((PIECES,)),
            sem((3,)),
            sem((3,)),
            sem((3,)),
            sem((2, PIECES)),
            sem((2, n_batch, PIECES)),
            sem((2, n_batch, PIECES)),
            sem((2, n_line, PIECES)),
            sem((2, 2, n_line, PIECES)),
            pltpu.VMEM((1, 1), f32),
        ],
        compiler_params=pltpu.CompilerParams(
            collective_id=0, has_side_effects=True, vmem_limit_bytes=VMEM_LIMIT
        ),
        name="block_step",
    )(activations, cotangent, weight, left_old, right_old)


ASSEMBLE_STEPS = 2


def assemble_kernel(
    left_own, right_own, direction_own, left_got, right_got, direction_got, first_in, second_in,
    first, left, right, direction, second,
):
    s = lax.axis_index("solver")
    width = direction_own.shape[1]
    for own, got, out in ((left_own, left_got, left), (right_own, right_got, right)):
        out[0, s] = own[...].astype(jnp.float32)
        out[0, 1 - s] = got[...].astype(jnp.float32)
    direction[:, pl.ds(pl.multiple_of(s * width, width), width)] = direction_own[...].astype(jnp.float32)
    direction[:, pl.ds(pl.multiple_of((1 - s) * width, width), width)] = direction_got[...].astype(jnp.float32)
    first[...] = first_in[...].T
    second[...] = second_in[...].T


def assemble(rows, first, second):
    half, width = rows[0].shape
    tokens, outs = first.shape
    step = half // ASSEMBLE_STEPS
    cols = outs // ASSEMBLE_STEPS
    f32 = jnp.float32
    part = pl.BlockSpec((step, width), lambda i: (i, 0))
    stat = pl.BlockSpec((1, 2, step, width), lambda i: (0, 0, i, 0))
    turned_in = pl.BlockSpec((tokens, cols), lambda i: (0, i))
    turned_out = pl.BlockSpec((cols, tokens), lambda i: (i, 0))
    return pl.pallas_call(
        assemble_kernel,
        grid=(ASSEMBLE_STEPS,),
        out_shape=(
            jax.ShapeDtypeStruct((outs, tokens), first.dtype),
            jax.ShapeDtypeStruct((1, 2, half, width), f32),
            jax.ShapeDtypeStruct((1, 2, half, width), f32),
            jax.ShapeDtypeStruct((half, 2 * width), f32),
            jax.ShapeDtypeStruct((outs, tokens), first.dtype),
        ),
        in_specs=[part] * 6 + [turned_in] * 2,
        out_specs=(turned_out, stat, stat, pl.BlockSpec((step, 2 * width), lambda i: (i, 0)), turned_out),
        compiler_params=pltpu.CompilerParams(vmem_limit_bytes=VMEM_LIMIT),
        name="assemble",
    )(*rows, first, second)


def owned_body(activations, cotangent, weight, left_old, right_old, *, n_batch, n_line):
    first, second, *rows = block_step(
        activations, cotangent, weight, left_old, right_old, n_batch, n_line
    )
    return assemble(rows, first, second)


def solution(mesh):
    in_specs = (
        P("batch", ("hidden", "solver")),
        P(("hidden", "solver"), "batch"),
        P(("hidden", "solver"), "batch"),
        P("hidden", "batch", None, None),
        P("hidden", "batch", None, None),
    )
    out_specs = (
        P(("hidden", "solver"), "batch"),
        P("hidden", "batch", "solver", None),
        P("hidden", "batch", "solver", None),
        P(("hidden", "solver"), "batch"),
        P(("hidden", "solver"), "batch"),
    )
    n_batch = mesh.shape["batch"]
    n_feat = mesh.shape["hidden"] * mesh.shape["solver"]

    n_line = mesh.shape["hidden"]
    n_solver = mesh.shape["solver"]

    def owned(activations, cotangent, weight, left_old, right_old):
        blocks = left_old.shape[1]
        even = n_line == n_batch == 2 * n_solver
        return even and n_solver == 2 and blocks == n_solver and cotangent.shape[0] == BLOCK

    def step(activations, cotangent, weight, left_old, right_old):
        args = (activations, cotangent, weight, left_old, right_old)
        if owned(*args):
            return owned_body(*args, n_batch=n_batch, n_line=n_line)
        return body(
            activations,
            cotangent,
            weight,
            left_old,
            right_old,
            n_batch=n_batch,
            n_solver=mesh.shape["solver"],
            n_feat=n_feat,
        )

    return jax.shard_map(step, mesh=mesh, in_specs=in_specs, out_specs=out_specs, check_vma=False)
```
